32 devices in a mesh: ctx: 16 (over z, x, core), head: 2 (over y).
Axes of the slice: x: 2, y: 2, z: 4, core: 2. Of those that a mesh axis runs over, the one named last changes fastest.
Arguments:
- query_rows: bfloat16 [8192, 2048], P('ctx', 'head'), may hold values from -60 to 60
- key_rows: bfloat16 [8192, 2048], P('ctx', 'head'), may hold values from -6 to 6
- value_rows: bfloat16 [8192, 2048], P('ctx', 'head'), may hold values from -60 to 60
- log_gate: float32 [16, 8192], P('head', 'ctx'), may hold values from -0.5 to 0
- conv_weight: float32 [3, 4, 2048], P(None, None, 'head'), may hold values from -3 to 3
- norm_gain: float32 [2048], P('head'), may hold values from 0.5 to 1.5
- mixed_grad: bfloat16 [8192, 2048], P('ctx', 'head'), may hold values from -24 to 24
Outputs:
- mixer_out: bfloat16 [8192, 2048], P('ctx', 'head')
- query_grad: bfloat16 [8192, 2048], P('ctx', 'head')
- key_grad: bfloat16 [8192, 2048], P('ctx', 'head')
- value_grad: bfloat16 [8192, 2048], P('ctx', 'head')
- conv_grad: float32 [3, 4, 2048], P(None, None, 'head')
- gain_grad: float32 [2048], P('head')
The draws below stay inside these ranges and needn't reach their ends.
All inputs are finite; a program needn't handle non-finite values.
Results may differ from the reference program's by a relative error of at most 0.015.
Values may be sent and summed in bfloat16 or wider, within the bound.
A program may use at most 128 MiB of HBM per device.

```python
import math
import jax
import jax.numpy as jnp
from jax import lax

HD = 128
HEADS = 16
TAPS = 4
GROUP = 512
D = 2048
TOKENS = 8192


def draw_query_rows(key, part):
    inner_key = jax.random.fold_in(key, 11)
    noise_key, scale_key = jax.random.split(inner_key)
    noise_part = jnp.clip(jax.random.normal(noise_key, (TOKENS, D), jnp.float32), -6.0, 6.0)
    scales = jnp.exp(jax.random.uniform(scale_key, (TOKENS, HEADS), jnp.float32, 0.0, math.log(10.0)))
    return (noise_part * jnp.repeat(scales, HD, axis=1)).astype(jnp.bfloat16)


def draw_value_rows(key, part):
    inner_key = jax.random.fold_in(key, 12)
    ramp = jnp.arange(HEADS).astype(jnp.float32) / (HEADS - 1)
    noise_part = jnp.clip(jax.random.normal(inner_key, (TOKENS, D), jnp.float32), -6.0, 6.0)
    scales = jnp.power(10.0, ramp)
    return (noise_part * jnp.repeat(scales, HD)[None, :]).astype(jnp.bfloat16)


def draw_mixed_grad(key, part):
    inner_key = jax.random.fold_in(key, 13)
    noise_key = jax.random.fold_in(inner_key, 0)
    ramp = jnp.arange(TOKENS).astype(jnp.float32) / (TOKENS - 1)
    noise_part = jnp.clip(jax.random.normal(noise_key, (TOKENS, D), jnp.float32), -6.0, 6.0)
    result = noise_part * jnp.power(3.0, ramp)[:, None]
    return result.astype(jnp.bfloat16)


def draw_log_gate(key, part):
    inner_key = jax.random.fold_in(key, 14)
    keys_all = jax.random.split(inner_key, 6)
    picker = jax.random.uniform(keys_all[0], (HEADS,), jnp.float32)
    is_fast = picker < 0.5
    slow_rate = jnp.exp(jax.random.uniform(keys_all[2], (HEADS,), jnp.float32, math.log(0.1), math.log(0.8))) / TOKENS
    fast_rate = jnp.exp(jax.random.uniform(keys_all[1], (HEADS,), jnp.float32, math.log(1.0 / 50.0), math.log(1.0 / 30.0)))
    head_rate = jnp.where(is_fast, fast_rate, slow_rate)
    jitter = jnp.exp(jax.random.uniform(keys_all[3], (HEADS, TOKENS), jnp.float32, math.log(0.5), math.log(2.0)))
    positions = jax.random.randint(keys_all[4], (3,), 0, TOKENS)
    hit_mask = jnp.any(jnp.arange(TOKENS)[None, :] == positions[:, None], axis=0)
    losses = jax.random.uniform(keys_all[5], (HEADS, TOKENS), jnp.float32, 0.2, 0.3)
    return -head_rate[:, None] * jitter + jnp.where(hit_mask[None, :], jnp.log(1.0 - losses), 0.0)


def steps_of(stream_key, dims, shards, low, top_value):
    def one(position, parts):
        heights = jax.random.uniform(jax.random.fold_in(jax.random.fold_in(stream_key, 6), position), (parts,), jnp.float32, low / len(shards), top_value / len(shards))
        return jnp.repeat(jnp.exp(heights), dims[position] // parts).reshape((-1,) + (1,) * (len(dims) - position - 1))

    gain = one(*shards[0])
    for cut in shards[1:]:
        gain = gain * one(*cut)
    return gain


def gaussian(own_key, dims, width, limit, pieces=(), kind=jnp.bfloat16):
    values = jax.random.normal(own_key, dims, jnp.float32) * width
    if len(pieces) > 0:
        values = steps_of(own_key, dims, pieces, -0.22, 0.18) * values
    return jnp.clip(values, min=-limit, max=limit).astype(kind)


def setup_inputs(seed: int = 0) -> dict:
    key_of = jax.random.split(jax.random.key(seed), 8)
    return {
        "query_rows": draw_query_rows(jax.random.fold_in(key_of[7], 71), 0),
        "key_rows": gaussian(key_of[1], (TOKENS, D), 1.0, 6.0, ((0, 16), (1, 2))),
        "value_rows": draw_value_rows(jax.random.fold_in(key_of[7], 71), 0),
        "log_gate": draw_log_gate(jax.random.fold_in(key_of[7], 71), 0),
        "conv_weight": gaussian(key_of[4], (3, TAPS, D), 0.5, 3.0, ((2, 2),), jnp.float32),
        "norm_gain": jnp.clip(1.0 + 0.1 * jax.random.normal(key_of[5], (D,), jnp.float32), 0.5, 1.5),
        "mixed_grad": draw_mixed_grad(jax.random.fold_in(key_of[7], 71), 0),
    }


norm_epsilon = 1e-05
highest = lax.Precision.HIGHEST

def lowered(values):
    return lax.optimization_barrier(values.astype(jnp.bfloat16)).astype(jnp.float32)

def conv_forward(rows, weight):
    wide = rows.astype(jnp.float32)
    result = weight[0][None, :] * wide
    for offset in range(1, TAPS):
        moved = jnp.concatenate([jnp.zeros((offset, wide.shape[1]), jnp.float32), wide[:-offset]], axis=0)
        result = result + weight[offset][None, :] * moved
    return result.astype(jnp.bfloat16)

def conv_backward(grad_rows, rows, weight):
    wide = rows.astype(jnp.float32)
    input_grad = weight[0][None, :] * grad_rows
    weight_grad = [lax.optimization_barrier(jnp.sum(grad_rows * wide, axis=0))]
    for offset in range(1, TAPS):
        ahead = jnp.concatenate([grad_rows[offset:], jnp.zeros((offset, wide.shape[1]), jnp.float32)], axis=0)
        input_grad = input_grad + weight[offset][None, :] * ahead
        behind = jnp.concatenate([jnp.zeros((offset, wide.shape[1]), jnp.float32), wide[:-offset]], axis=0)
        weight_grad.append(lax.optimization_barrier(jnp.sum(grad_rows * behind, axis=0)))
    return (input_grad.astype(jnp.bfloat16), jnp.stack(weight_grad))

def decay_tables(gate_blocks):
    running = jnp.cumsum(gate_blocks, axis=-1)
    closing = running[..., -1]
    gap_matrix = running[..., :, None] - running[..., None, :]
    block_size = gate_blocks.shape[-1]
    lower_mask = jnp.arange(block_size)[:, None] >= jnp.arange(block_size)[None, :]
    weights = jnp.where(lower_mask, jnp.exp(jnp.minimum(gap_matrix, 0.0)), 0.0)
    return (running, closing, weights)

def reference(query_rows, key_rows, value_rows, log_gate, conv_weight, norm_gain, mixed_grad):
    query_conv = conv_forward(query_rows, conv_weight[0])
    key_conv = conv_forward(key_rows, conv_weight[1])
    value_conv = conv_forward(value_rows, conv_weight[2])
    block_count = TOKENS // GROUP

    def blocked(rows):
        return rows.astype(jnp.float32).reshape(block_count, GROUP, HEADS, HD)
    query_blocks = blocked(query_conv)
    key_blocks = blocked(key_conv)
    value_blocks = blocked(value_conv)
    gate_blocks = log_gate.reshape(HEADS, block_count, GROUP).transpose(1, 0, 2)

    def forward_step(state, inputs):
        query_here, key_here, value_here, gate_here = inputs
        running, closing, weights = decay_tables(gate_here)
        grow_factor = jnp.exp(running).T[:, :, None]
        shrink = jnp.exp(closing[:, None] - running).T[:, :, None]
        scores = jnp.einsum('thd,shd->hts', query_here, key_here, precision=highest)
        weights_low = lowered(scores * weights)
        state_low = lowered(state)
        attended = jnp.einsum('hts,she->the', weights_low, value_here, precision=highest)
        attended = attended + jnp.einsum('thd,hde->the', query_here, state_low, precision=highest) * grow_factor
        key_scaled = lowered(key_here * shrink)
        new_state = jnp.exp(closing)[:, None, None] * state + jnp.einsum('shd,she->hde', key_scaled, value_here, precision=highest)
        return (new_state, (attended, state))
    zero_state = jnp.zeros((HEADS, HD, HD), jnp.float32)
    last_state, (attended, states_in) = lax.scan(forward_step, zero_state, (query_blocks, key_blocks, value_blocks, gate_blocks))
    attended = attended.reshape(TOKENS, D)
    inverse = lax.rsqrt(lax.optimization_barrier(jnp.mean(attended * attended, axis=1)) + norm_epsilon)
    normed = attended * inverse[:, None]
    mixer_out = (normed * norm_gain[None, :]).astype(jnp.bfloat16)
    grad_wide = mixed_grad.astype(jnp.float32)
    gain_grad = lax.optimization_barrier(jnp.sum(grad_wide * normed, axis=0))
    scaled = grad_wide * norm_gain[None, :]
    inner_sum = lax.optimization_barrier(jnp.mean(scaled * attended, axis=1))
    out_grad = (inverse[:, None] * (scaled - attended * (inverse * inverse * inner_sum)[:, None])).astype(jnp.bfloat16)
    grad_blocks = blocked(out_grad)

    def backward_step(later_state, inputs):
        query_here, key_here, value_here, grad_here, gate_here, state_here = inputs
        running, closing, weights = decay_tables(gate_here)
        grow_factor = jnp.exp(running).T[:, :, None]
        shrink = jnp.exp(closing[:, None] - running).T[:, :, None]
        scores = jnp.einsum('thd,shd->hts', query_here, key_here, precision=highest)
        weights_low = lowered(scores * weights)
        state_low = lowered(state_here)
        later_low = lowered(later_state)
        grad_scores = lowered(jnp.einsum('the,she->hts', grad_here, value_here, precision=highest) * weights)
        query_part = jnp.einsum('hts,shd->thd', grad_scores, key_here, precision=highest)
        query_part = query_part + jnp.einsum('the,hde->thd', grad_here, state_low, precision=highest) * grow_factor
        key_part = jnp.einsum('hts,thd->shd', grad_scores, query_here, precision=highest)
        key_part = key_part + jnp.einsum('she,hde->shd', value_here, later_low, precision=highest) * shrink
        value_part = jnp.einsum('hts,the->she', weights_low, grad_here, precision=highest)
        value_part = value_part + jnp.einsum('shd,hde->she', key_here, later_low, precision=highest) * shrink
        query_scaled = lowered(query_here * grow_factor)
        new_later = jnp.exp(closing)[:, None, None] * later_state + jnp.einsum('thd,the->hde', query_scaled, grad_here, precision=highest)
        return (new_later, (query_part, key_part, value_part))
    first_later, (query_cg, key_cg, value_cg) = lax.scan(backward_step, zero_state, (query_blocks, key_blocks, value_blocks, grad_blocks, gate_blocks, states_in), reverse=True)
    query_grad, query_taps = conv_backward(query_cg.reshape(TOKENS, D), query_rows, conv_weight[0])
    key_grad, key_taps = conv_backward(key_cg.reshape(TOKENS, D), key_rows, conv_weight[1])
    value_grad, value_taps = conv_backward(value_cg.reshape(TOKENS, D), value_rows, conv_weight[2])
    conv_grad = jnp.stack([query_taps, key_taps, value_taps])
    return (mixer_out, query_grad, key_grad, value_grad, conv_grad, gain_grad)
```

```python
import functools

import jax
import jax.numpy as jnp
from jax import lax
from jax.experimental import pallas as pl
from jax.experimental.pallas import tpu as pltpu
from jax.sharding import PartitionSpec as P

HD = 128
TAPS = 4
GROUP = 512
HALF = GROUP // 2
UNROLL = 8
SEG = HALF // 8
LEAD = 8 * (TAPS - 1)
EDGE = 16
EPS = 1e-05
MESH = pl.DeviceIdType.MESH
F32 = jnp.float32
BF16 = jnp.bfloat16


def dot_nn(a, b):
    return lax.dot_general(a, b, (((1,), (0,)), ((), ())), preferred_element_type=F32)


def dot_nt(a, b):
    return lax.dot_general(a, b, (((1,), (1,)), ((), ())), preferred_element_type=F32)


def dot_tn(a, b):
    return lax.dot_general(a, b, (((0,), (0,)), ((), ())), preferred_element_type=F32)


def times(shape, axis):
    p = lax.broadcasted_iota(jnp.int32, shape, axis)
    return (p & 7) * SEG + (p >> 3)


def kernel(
    n, m, heads, owners,
    q_hbm, k_hbm, v_hbm, g_hbm, lg_hbm, w_hbm, gain_hbm,
    mix_ref, qg_ref, kg_ref, vg_ref, cgrad_ref, ggrad_ref,
    ext, hal, lg_ref, w_ref, gain_ref, perm,
    xf, qc, kc, vc, gf, att, og, mixb, cg, etx, erx,
    w0, w1, p0, p1, colb, rowb, closb, closr,
    fs, fr, fo, fi, bs, br, bo, bi,
    accs, acci, invb, coefb, hs_tx, hs_rx,
    tap, tapr, tsum, tapo,
    loc, ha_s, ha_r, cl_s, cl_r,
    f1_s, f1_r, f2_s, f2_r, b1_s, b1_r, b2_s, b2_r,
    hs_s, hs_r, eh_s, eh_r, t1_s, t1_r, t2_s, t2_r,
):
    me = lax.axis_index("ctx")
    hme = lax.axis_index("head")
    per = owners // heads
    R = HD // per
    tiles = 2 * heads
    width = heads * HD
    total = width * m
    convs = (qc, kc, vc)
    chunk = min(2 * HD, width)

    def ctx_copy(src, dst, ss, rs, p):
        return pltpu.make_async_remote_copy(
            src_ref=src, dst_ref=dst, send_sem=ss, recv_sem=rs,
            device_id={"ctx": p}, device_id_type=MESH,
        )

    def head_copy(src, dst, ss, rs, p):
        return pltpu.make_async_remote_copy(
            src_ref=src, dst_ref=dst, send_sem=ss, recv_sem=rs,
            device_id={"head": p}, device_id_type=MESH,
        )

    def peers(count, fn):
        def one(d, c):
            p = lax.rem(me + d, n)
            if count == n:
                fn(p)
            else:
                pl.when(p < count)(lambda: fn(p))
            return c

        lax.fori_loop(1, n, one, 0)

    def owning(count, fn):
        if count == n:
            fn()
        else:
            pl.when(me < count)(fn)

    def cols_of(h):
        if isinstance(h, int):
            return pl.ds(h * HD, HD)
        return pl.ds(pl.multiple_of(h * HD, HD), HD)

    def over(lo, hi, fn):
        k = min(UNROLL, hi - lo)
        if k == hi - lo:
            for h in range(lo, hi):
                fn(h, 0)
        else:

            def some(i, c):
                for u in range(k):
                    fn(lo + i * k + u, 0)
                return c

            lax.fori_loop(0, (hi - lo) // k, some, 0)

    ins = [
        pltpu.make_async_copy(src, dst, loc.at[i])
        for i, (src, dst) in enumerate((
            (lg_hbm, lg_ref), (k_hbm, ext.at[1]), (v_hbm, ext.at[2]),
            (w_hbm, w_ref), (q_hbm, ext.at[0]), (g_hbm, ext.at[3]), (gain_hbm, gain_ref),
        ))
    ]
    for cp in ins:
        cp.start()

    barrier = pltpu.get_barrier_semaphore()

    def greet(p):
        pl.semaphore_signal(barrier, inc=1, device_id={"ctx": p}, device_id_type=MESH)

    peers(n, greet)
    for d in range(1, m):
        pl.semaphore_signal(
            barrier, inc=1, device_id={"head": lax.rem(hme + d, m)}, device_id_type=MESH
        )

    at = times((HALF, HALF), 0)
    along = times((HALF, HALF), 1)
    row_id = lax.broadcasted_iota(jnp.int32, (HALF, HALF), 0)
    lane_id = lax.broadcasted_iota(jnp.int32, (HALF, HALF), 1)
    perm[0] = jnp.where(at == lane_id, 1.0, 0.0).astype(BF16)
    perm[1] = jnp.where(row_id == along, 1.0, 0.0).astype(BF16)

    tap[...] = jnp.zeros_like(tap)
    hs_tx[...] = jnp.zeros_like(hs_tx)
    etx[...] = jnp.zeros_like(etx)

    ins[0].wait()
    gate = lg_ref[...]
    high = gate.astype(BF16).astype(F32)
    rest = gate - high
    mid_ = rest.astype(BF16).astype(F32)
    parts = (high, mid_, rest - mid_)
    stacked = jnp.concatenate(
        [x[:, :HALF] for x in parts] + [x[:, HALF:] for x in parts], axis=0
    ).astype(BF16)
    upto = jnp.where(row_id <= along, 1.0, 0.0).astype(BF16)
    sums_ = dot_nn(stacked, upto)
    run0 = sums_[0:8] + sums_[8:16] + sums_[16:24]
    run1 = sums_[24:32] + sums_[32:40] + sums_[40:48] + run0[:, HALF - 1 : HALF]
    run = jnp.concatenate([run0, run1], axis=1)
    run_t = run.T
    for h in range(heads):
        colb[h] = jnp.broadcast_to(run_t[:, h : h + 1], (GROUP, HD))
        rowb[h] = jnp.broadcast_to(run[h : h + 1, :], (8, GROUP))
        closb[h] = jnp.broadcast_to(run[h : h + 1, GROUP - 1 : GROUP], (8, HD))

    pl.semaphore_wait(barrier, n - 1 + m - 1)

    def halo(c):
        return ctx_copy(
            (q_hbm, k_hbm, v_hbm)[c].at[pl.ds(GROUP - EDGE, EDGE), :], hal.at[c],
            ha_s.at[c], ha_r.at[c], lax.rem(me + 1, n),
        )

    @pl.when(me < n - 1)
    def _():
        for c in (1, 2, 0):
            halo(c).start()

    @pl.when(me == 0)
    def _():
        hal[...] = jnp.zeros_like(hal)

    def clos_copy(p, source):
        return ctx_copy(closb.at[p // per], closr.at[source], cl_s.at[p], cl_r.at[source], p)

    peers(owners, lambda p: clos_copy(p, me).start())

    def own_clos():
        closr[me] = closb[me // per]

    owning(owners, own_clos)

    def decay(h, c):
        col = colb[h]
        row = rowb[h][0:1, :]
        top = jnp.concatenate([col[:HALF]] * 2, axis=1)
        low = jnp.concatenate([col[HALF:]] * 2, axis=1)
        keep = times((HALF, HALF), 0) >= times((HALF, HALF), 1)
        w0[h] = jnp.where(keep, jnp.exp(jnp.minimum(top - row[:, :HALF], 0.0)), 0.0)
        w1[h, :, :HALF] = jnp.exp(jnp.minimum(low - row[:, :HALF], 0.0))
        w1[h, :, HALF:] = jnp.where(keep, jnp.exp(jnp.minimum(low - row[:, HALF:], 0.0)), 0.0)
        return c

    over(0, heads, decay)

    def spread(c, i, dst):
        ins[i].wait()
        for half in range(2):
            for k in range(0, width, chunk):
                cols = pl.ds(k, chunk)
                dst(half)[:, cols] = dot_nn(perm[0], ext[c, pl.ds(half * HALF, HALF), cols])

    def gather(src):
        return dot_nn(perm[1], src).astype(BF16)

    first = lax.broadcasted_iota(jnp.int32, (8, width), 0) == 0
    last = lax.broadcasted_iota(jnp.int32, (8, width), 0) == 7

    def lead(c):
        edge_rows = hal[c].astype(F32)
        for j in range(1, TAPS):
            r = LEAD + HALF - 8 * j
            before = jnp.broadcast_to(edge_rows[EDGE - j : EDGE - j + 1], (8, width))
            for half in range(2):
                block = xf[c, half, pl.ds(r, 8), :]
                moved = pltpu.roll(block, 1, 0)
                xf[c, half, pl.ds(LEAD - 8 * j, 8), :] = jnp.where(first, before, moved)
                before = moved

    def half_of(c):
        return lambda half: xf.at[c, half, pl.ds(LEAD, HALF), :]

    spread(1, 1, half_of(1))
    spread(2, 2, half_of(2))
    ins[3].wait()

    @pl.when(me > 0)
    def _():
        for c in range(3):
            halo(c).wait_recv()

    lead(1)
    lead(2)

    def conv(c, h):
        cols = cols_of(h)
        for half in range(2):
            y = w_ref[c, 0:1, cols] * xf[c, half, pl.ds(LEAD, HALF), cols]
            for j in range(1, TAPS):
                y = y + w_ref[c, j : j + 1, cols] * xf[c, half, pl.ds(LEAD - 8 * j, HALF), cols]
            convs[c][pl.ds(half * HALF, HALF), cols] = y.astype(BF16)

    def shrink_of(h):
        return jnp.exp(closb[h][0:1, :] - colb[h])

    def slice_copy(src, dst, ss, rs, o, source):
        return ctx_copy(src.at[o], dst.at[source], ss.at[o], rs.at[source], o)

    def keep_slices(state, h, src):
        state = state.astype(BF16)
        for i in range(per):
            src[h * per + i] = state[i * R : (i + 1) * R]

    def hand_out(lo, hi, src, dst, ss, rs):
        span = (hi - lo) * per

        def one(d, c):
            o = lo * per + lax.rem(d + me, span)

            @pl.when(o != me)
            def _():
                slice_copy(src, dst, ss, rs, o, me).start()

            @pl.when(o == me)
            def _():
                dst[me] = src[me]

            return c

        lax.fori_loop(0, span, one, 0)

    def scan_slices(backwards, src, ss, got, rs, out, res, ss2, rs2):
        def take():
            peers(n, lambda s: slice_copy(src, got, ss, rs, 0, s).wait_recv())

            def step(i, state):
                b = n - 1 - i if backwards else i
                out[b] = state.astype(BF16)
                return jnp.exp(closr[b][0:1, :]) * state + got[b].astype(F32)

            lax.fori_loop(0, n, step, jnp.zeros((R, HD), F32))
            peers(n, lambda p: ctx_copy(out.at[p], res.at[me], ss2.at[p], rs2.at[me], p).start())
            res[me] = out[me]

        owning(owners, take)

    def await_states(out, res, ss2, rs2):
        peers(owners, lambda o: ctx_copy(out.at[0], res.at[o], ss2.at[0], rs2.at[o], o).wait_recv())

    def state_of(res, h):
        return res[pl.ds(h * per, per)].reshape(HD, HD)

    def local_state(h, c):
        cols = cols_of(h)
        conv(1, h)
        conv(2, h)
        ks = (kc[:, cols].astype(F32) * shrink_of(h)).astype(BF16)
        keep_slices(dot_tn(ks, vc[:, cols]), h, fs)
        return c

    mid = heads // 2
    over(0, mid, local_state)
    hand_out(0, mid, fs, fr, f1_s, f1_r)
    over(mid, heads, local_state)
    hand_out(mid, heads, fs, fr, f1_s, f1_r)

    spread(0, 4, half_of(0))
    lead(0)
    spread(3, 5, lambda half: gf.at[pl.ds(half * HALF, HALF), :])
    ins[6].wait()

    def inner(h, c):
        cols = cols_of(h)
        conv(0, h)
        q0, q1 = qc[:HALF, cols], qc[HALF:, cols]
        a0 = (dot_nt(q0, kc[:HALF, cols]) * w0[h]).astype(BF16)
        a1 = (dot_nt(q1, kc[:, cols]) * w1[h]).astype(BF16)
        p0[h] = a0
        p1[h] = a1
        att[:HALF, cols] = dot_nn(a0, vc[:HALF, cols])
        att[HALF:, cols] = dot_nn(a1, vc[:, cols])
        return c

    over(0, mid, inner)

    def clos_in():
        peers(n, lambda s: clos_copy(me, s).wait_recv())

    owning(owners, clos_in)
    scan_slices(False, fs, f1_s, fr, f1_r, fo, fi, f2_s, f2_r)
    over(mid, heads, inner)
    await_states(fo, fi, f2_s, f2_r)

    accs[...] = jnp.zeros_like(accs)
    acci[...] = jnp.zeros_like(acci)

    def outer(h, c):
        cols = cols_of(h)
        a = att[:, cols] + dot_nn(qc[:, cols], state_of(fi, h)) * jnp.exp(colb[h])
        att[:, cols] = a
        accs[...] += a * a
        acci[...] += gf[:, cols] * gain_ref[0:1, cols] * a
        return c

    over(0, heads, outer)
    hs_tx[0:1, :] = jnp.sum(accs[...].T, axis=0, keepdims=True)
    hs_tx[1:2, :] = jnp.sum(acci[...].T, axis=0, keepdims=True)

    def sums_copy(p, source):
        return head_copy(hs_tx, hs_rx.at[source], hs_s.at[p], hs_r.at[source], p)

    for d in range(1, m):
        sums_copy(lax.rem(hme + d, m), hme).start()
    hs_rx[hme] = hs_tx[...]
    for d in range(1, m):
        sums_copy(hme, lax.rem(hme + d, m)).wait_recv()
    sums = hs_rx[0]
    for d in range(1, m):
        sums = sums + hs_rx[d]
    inverse = lax.rsqrt(sums[0:1, :] / total + EPS)
    coef = inverse * inverse * (sums[1:2, :] / total)
    both = jnp.concatenate([inverse, coef, jnp.zeros((6, GROUP), F32)], axis=0).T
    invb[...] = jnp.broadcast_to(both[:, 0:1], (GROUP, HD))
    coefb[...] = jnp.broadcast_to(both[:, 1:2], (GROUP, HD))

    def norm(h, c):
        cols = cols_of(h)
        a = att[:, cols]
        inv = invb[...]
        normed = a * inv
        gain = gain_ref[0:1, cols]
        gw = gf[:, cols]
        mixb[:, cols] = (normed * gain).astype(BF16)
        tap[heads + h, 4:5, :] = jnp.sum(gw * normed, axis=0, keepdims=True)
        o = (inv * (gw * gain - a * coefb[...])).astype(BF16)
        og[:, cols] = o
        qs = (qc[:, cols].astype(F32) * jnp.exp(colb[h])).astype(BF16)
        keep_slices(dot_tn(qs, o), h, bs)
        return c

    over(0, mid, norm)
    hand_out(0, mid, bs, br, b1_s, b1_r)
    over(mid, heads, norm)
    hand_out(mid, heads, bs, br, b1_s, b1_r)
    def back(h, c):
        cols = cols_of(h)
        o0, o1 = og[:HALF, cols], og[HALF:, cols]
        s0 = (dot_nt(o0, vc[:HALF, cols]) * w0[h]).astype(BF16)
        s1 = (dot_nt(o1, vc[:, cols]) * w1[h]).astype(BF16)
        through = dot_nt(og[:, cols], state_of(fi, h)) * jnp.exp(colb[h])
        cg[0, 0, :HALF, cols] = dot_nn(s0, kc[:HALF, cols]) + through[:HALF]
        cg[0, 1, :HALF, cols] = dot_nn(s1, kc[:, cols]) + through[HALF:]
        kk = dot_tn(s1, qc[HALF:, cols])
        cg[1, 0, :HALF, cols] = kk[:HALF] + dot_tn(s0, qc[:HALF, cols])
        cg[1, 1, :HALF, cols] = kk[HALF:]
        vv = dot_tn(p1[h], o1)
        cg[2, 0, :HALF, cols] = vv[:HALF] + dot_tn(p0[h], o0)
        cg[2, 1, :HALF, cols] = vv[HALF:]
        return c

    over(0, mid, back)
    scan_slices(True, bs, b1_s, br, b1_r, bo, bi, b2_s, b2_r)
    over(mid, heads, back)

    for half in range(2):
        for k in range(0, width, chunk):
            cols = pl.ds(k, chunk)
            rows = pl.ds(half * HALF, HALF)
            mix_ref[rows, cols] = gather(mixb[rows, cols])

    def edge(c):
        return ctx_copy(
            etx.at[c], erx.at[c], eh_s.at[c], eh_r.at[c], lax.rem(me + n - 1, n)
        )

    def send_edge(c):
        for j in range(TAPS - 1):
            etx[c, j : j + 1, :] = cg[c, 0, pl.ds(8 * j, 1), :]

        @pl.when(me > 0)
        def _():
            edge(c).start()

    @pl.when(me == n - 1)
    def _():
        erx[...] = jnp.zeros_like(erx)

    send_edge(0)

    def taps(c, h):
        cols = cols_of(h)
        for j in range(TAPS):
            r = c * TAPS + j
            total_ = 0.0
            for half in range(2):
                total_ = total_ + jnp.sum(
                    cg[c, half, pl.ds(0, HALF), cols]
                    * xf[c, half, pl.ds(LEAD - 8 * j, HALF), cols],
                    axis=0, keepdims=True,
                )
            tap[(r // 8) * heads + h, r % 8 : r % 8 + 1, :] = total_

    def q_taps(h, c):
        taps(0, h)
        return c

    over(0, heads, q_taps)
    await_states(bo, bi, b2_s, b2_r)

    def late(h, c):
        cols = cols_of(h)
        state = state_of(bi, h)
        sh = shrink_of(h)
        for i, add in ((1, dot_nt(vc[:, cols], state) * sh), (2, dot_nn(kc[:, cols], state) * sh)):
            cg[i, 0, :HALF, cols] += add[:HALF]
            cg[i, 1, :HALF, cols] += add[HALF:]
        return c

    over(0, heads, late)

    send_edge(1)
    send_edge(2)

    def kv_taps(h, c):
        taps(1, h)
        taps(2, h)
        return c

    over(0, heads, kv_taps)

    def tap_copy(o, source):
        return ctx_copy(tap.at[o], tapr.at[source], t1_s.at[o], t1_r.at[source], o)

    peers(tiles, lambda o: tap_copy(o, me).start())

    @pl.when(me < n - 1)
    def _():
        for c in range(3):
            edge(c).wait_recv()

    def unconv(c):
        for j in range(TAPS - 1):
            after = jnp.broadcast_to(erx[c, j : j + 1, :], (8, width))
            for half in (1, 0):
                moved = pltpu.roll(cg[c, half, pl.ds(8 * j, 8), :], 7, 0)
                cg[c, half, pl.ds(HALF + 8 * j, 8), :] = jnp.where(last, after, moved)
                after = moved
        for half in range(2):
            for k in range(0, width, chunk):
                cols = pl.ds(k, chunk)
                y = w_ref[c, 0:1, cols] * cg[c, half, pl.ds(0, HALF), cols]
                for j in range(1, TAPS):
                    y = y + w_ref[c, j : j + 1, cols] * cg[c, half, pl.ds(8 * j, HALF), cols]
                outs[c][pl.ds(half * HALF, HALF), cols] = gather(y.astype(BF16))

    outs = (qg_ref, kg_ref, vg_ref)
    unconv(0)

    def sum_copy(p, source):
        return ctx_copy(tsum, tapo.at[source], t2_s.at[p], t2_r.at[source], p)

    def own_sum():
        tapr[me] = tap[me]
        peers(n, lambda s: tap_copy(0, s).wait_recv())
        tsum[...] = lax.fori_loop(0, n, lambda s, a: a + tapr[s], jnp.zeros((8, HD), F32))
        tapo[me] = tsum[...]
        peers(n, lambda p: sum_copy(p, me).start())

    owning(tiles, own_sum)
    unconv(1)
    unconv(2)
    peers(tiles, lambda o: sum_copy(0, o).wait_recv())
    for h in range(heads):
        cols = slice(h * HD, (h + 1) * HD)
        low, high = tapo[h], tapo[heads + h]
        cgrad_ref[0, :, cols] = low[0:4]
        cgrad_ref[1, :, cols] = low[4:8]
        cgrad_ref[2, :, cols] = high[0:4]
        ggrad_ref[0:1, cols] = high[4:5]

    @pl.when(me < n - 1)
    def _():
        for c in range(3):
            halo(c).wait_send()

    @pl.when(me > 0)
    def _():
        for c in range(3):
            edge(c).wait_send()

    def sent_to_owner(o):
        clos_copy(o, me).wait_send()
        slice_copy(fs, fr, f1_s, f1_r, o, me).wait_send()
        slice_copy(bs, br, b1_s, b1_r, o, me).wait_send()

    peers(owners, sent_to_owner)

    def sent_states():
        def one(p):
            ctx_copy(fo.at[p], fi.at[me], f2_s.at[p], f2_r.at[me], p).wait_send()
            ctx_copy(bo.at[p], bi.at[me], b2_s.at[p], b2_r.at[me], p).wait_send()

        peers(n, one)

    owning(owners, sent_states)
    for d in range(1, m):
        sums_copy(lax.rem(hme + d, m), hme).wait_send()
    peers(tiles, lambda o: tap_copy(o, me).wait_send())
    owning(tiles, lambda: peers(n, lambda p: sum_copy(p, me).wait_send()))


def hand_on(*refs):
    count = (len(refs) - 1) // 2
    put = refs[-1]
    moves = [
        pltpu.make_async_copy(refs[i], refs[count + i], put.at[i]) for i in range(count)
    ]
    for cp in moves:
        cp.start()
    for cp in moves:
        cp.wait()


def body(n, m, query_rows, key_rows, value_rows, log_gate, conv_weight, norm_gain, mixed_grad):
    tok_here, width = query_rows.shape
    assert tok_here == GROUP
    heads = width // HD
    owners = min(n, width // 16)
    per = owners // heads
    R = HD // per
    tiles = 2 * heads
    assert tiles <= n
    if heads < 8:
        log_gate = jnp.pad(log_gate, ((0, 8 - heads), (0, 0)))
    any_ = pl.BlockSpec(memory_space=pl.ANY)
    vm = pl.BlockSpec(memory_space=pltpu.VMEM)
    V = pltpu.VMEM
    S = pltpu.SemaphoreType.DMA
    hbm = pl.BlockSpec(memory_space=pltpu.HBM)
    result = pl.pallas_call(
        functools.partial(kernel, n, m, heads, owners),
        out_shape=(
            V((GROUP, width), BF16), V((GROUP, width), BF16),
            V((GROUP, width), BF16), V((GROUP, width), BF16),
            V((3, TAPS, width), F32), V((1, width), F32),
        ),
        in_specs=[hbm] * 7,
        out_specs=(vm,) * 6,
        scratch_shapes=[
            V((4, GROUP, width), BF16),
            V((3, EDGE, width), BF16),
            V((8, GROUP), F32),
            V((3, TAPS, width), F32),
            V((1, width), F32),
            V((2, HALF, HALF), BF16),
            V((3, 2, LEAD + HALF, width), F32),
            V((GROUP, width), BF16),
            V((GROUP, width), BF16),
            V((GROUP, width), BF16),
            V((GROUP, width), F32),
            V((GROUP, width), F32),
            V((GROUP, width), BF16),
            V((GROUP, width), BF16),
            V((3, 2, HALF + LEAD, width), F32),
            V((3, 8, width), F32),
            V((3, 8, width), F32),
            V((heads, HALF, HALF), F32),
            V((heads, HALF, GROUP), F32),
            V((heads, HALF, HALF), BF16),
            V((heads, HALF, GROUP), BF16),
            V((heads, GROUP, HD), F32),
            V((heads, 8, GROUP), F32),
            V((heads, 8, HD), F32),
            V((n, 8, HD), F32),
            V((owners, R, HD), BF16),
            V((n, R, HD), BF16),
            V((n, R, HD), BF16),
            V((owners, R, HD), BF16),
            V((owners, R, HD), BF16),
            V((n, R, HD), BF16),
            V((n, R, HD), BF16),
            V((owners, R, HD), BF16),
            V((GROUP, HD), F32),
            V((GROUP, HD), F32),
            V((GROUP, HD), F32),
            V((GROUP, HD), F32),
            V((8, GROUP), F32),
            V((m, 8, GROUP), F32),
            V((tiles, 8, HD), F32),
            V((n, 8, HD), F32),
            V((8, HD), F32),
            V((tiles, 8, HD), F32),
            S((8,)), S((3,)), S((3,)), S((n,)), S((n,)),
            S((n,)), S((n,)), S((n,)), S((n,)),
            S((n,)), S((n,)), S((n,)), S((n,)),
            S((m,)), S((m,)), S((3,)), S((3,)),
            S((n,)), S((n,)), S((n,)), S((n,)),
        ],
        compiler_params=pltpu.CompilerParams(
            collective_id=0, has_side_effects=True, vmem_limit_bytes=52 * 1024 * 1024
        ),
    )(
        query_rows, key_rows, value_rows, mixed_grad,
        log_gate, conv_weight, norm_gain.reshape(1, width),
    )
    result = pl.pallas_call(
        hand_on,
        out_shape=tuple(jax.ShapeDtypeStruct(r.shape, r.dtype) for r in result),
        in_specs=[any_] * 6,
        out_specs=(any_,) * 6,
        scratch_shapes=[S((6,))],
        compiler_params=pltpu.CompilerParams(vmem_limit_bytes=4 * 1024 * 1024),
    )(*result)
    return (*result[:5], result[5].reshape(width))


def solution(mesh):
    n, m = mesh.shape["ctx"], mesh.shape["head"]
    rows = P("ctx", "head")
    return jax.shard_map(
        functools.partial(body, n, m),
        mesh=mesh,
        in_specs=(rows, rows, rows, P("head", "ctx"), P(None, None, "head"), P("head"), rows),
        out_specs=(rows, rows, rows, rows, P(None, None, "head"), P("head")),
        check_vma=False,
    )
```

```python
import functools

import jax
import jax.numpy as jnp
from jax import lax
from jax.experimental import pallas as pl
from jax.experimental.pallas import tpu as pltpu
from jax.sharding import PartitionSpec as P

HD = 128
TAPS = 4
GROUP = 512
HALF = GROUP // 2
UNROLL = 8
SEG = HALF // 8
LEAD = 8 * (TAPS - 1)
EDGE = 16
FIX = 32
EPS = 1e-05
MESH = pl.DeviceIdType.MESH
F32 = jnp.float32
BF16 = jnp.bfloat16


def dot_nn(a, b):
    return lax.dot_general(a, b, (((1,), (0,)), ((), ())), preferred_element_type=F32)


def dot_nt(a, b):
    return lax.dot_general(a, b, (((1,), (1,)), ((), ())), preferred_element_type=F32)


def dot_tn(a, b):
    return lax.dot_general(a, b, (((0,), (0,)), ((), ())), preferred_element_type=F32)


def times(shape, axis):
    p = lax.broadcasted_iota(jnp.int32, shape, axis)
    return (p & 7) * SEG + (p >> 3)


def kernel(
    n, m, heads, owners,
    q_hbm, k_hbm, v_hbm, g_hbm, lg_hbm, w_hbm, gain_hbm,
    mix_ref, qg_ref, kg_ref, vg_ref, cgrad_ref, ggrad_ref,
    ext, hal, lg_ref, w_ref, gain_ref, perm,
    xf, qc, kc, vc, gf, att, og, mixb, cg, etx, erx,
    w0, w1, p0, p1, colb, rowb, closb, closp, closc, closr,
    local, fx_t, fx_r, fs, fr, fo, fi, fp, fin,
    bx_t, bx_r, bs, br, bo, bi, bp, bin_,
    accs, acci, invb, coefb, hs_tx, hs_rx,
    tap, tapp, tapb, tapr,
    loc, ha_s, ha_r, cp_s, cp_r, cl_s, cl_r,
    fx_s, fx_q, f1_s, f1_r, f2_s, f2_r, fp_s, fp_r,
    bx_s, bx_q, b1_s, b1_r, b2_s, b2_r, bp_s, bp_r,
    hs_s, hs_r, eh_s, eh_r, tp_s, tp_r, t_s, t_r,
):
    me = lax.axis_index("ctx")
    hme = lax.axis_index("head")
    chips = n // 2
    chip = me // 2
    core = lax.rem(me, 2)
    partner = me + 1 - 2 * core
    beyond = lax.rem(me + n - 1 + 2 * core, n)
    hc = heads // 2
    mine = core * hc
    theirs = hc - mine
    per = owners // hc
    R = HD // per
    width = heads * HD
    total = width * m
    convs = (qc, kc, vc)
    chunk = min(2 * HD, width)

    def ctx_copy(src, dst, ss, rs, p):
        return pltpu.make_async_remote_copy(
            src_ref=src, dst_ref=dst, send_sem=ss, recv_sem=rs,
            device_id={"ctx": p}, device_id_type=MESH,
        )

    def head_copy(src, dst, ss, rs, p):
        return pltpu.make_async_remote_copy(
            src_ref=src, dst_ref=dst, send_sem=ss, recv_sem=rs,
            device_id={"head": p}, device_id_type=MESH,
        )

    def peers(count, fn):
        def one(d, c):
            p = lax.rem(chip + d, chips)
            if count == chips:
                fn(p)
            else:
                pl.when(p < count)(lambda: fn(p))
            return c

        lax.fori_loop(1, chips, one, 0)

    def owning(fn):
        if owners == chips:
            fn()
        else:
            pl.when(chip < owners)(fn)

    def cols_of(h):
        if isinstance(h, int):
            return pl.ds(h * HD, HD)
        return pl.ds(pl.multiple_of(h * HD, HD), HD)

    def over(lo, hi, fn):
        for h in range(lo, hi):
            fn(h, 0)

    def group(first, fn):
        for i in range(hc):
            fn(first + i, i)

    ins = [
        pltpu.make_async_copy(src, dst, loc.at[i])
        for i, (src, dst) in enumerate((
            (lg_hbm, lg_ref), (k_hbm, ext.at[1]), (v_hbm, ext.at[2]),
            (w_hbm, w_ref), (q_hbm, ext.at[0]), (g_hbm, ext.at[3]), (gain_hbm, gain_ref),
        ))
    ]
    for cp in ins:
        cp.start()

    barrier = pltpu.get_barrier_semaphore()

    def greet(p):
        pl.semaphore_signal(barrier, inc=1, device_id={"ctx": p}, device_id_type=MESH)

    greet(beyond)
    peers(chips, lambda p: greet(2 * p + core))
    greet(partner)
    for d in range(1, m):
        pl.semaphore_signal(
            barrier, inc=1, device_id={"head": lax.rem(hme + d, m)}, device_id_type=MESH
        )

    at = times((HALF, HALF), 0)
    along = times((HALF, HALF), 1)
    row_id = lax.broadcasted_iota(jnp.int32, (HALF, HALF), 0)
    lane_id = lax.broadcasted_iota(jnp.int32, (HALF, HALF), 1)
    perm[0] = jnp.where(at == lane_id, 1.0, 0.0).astype(BF16)
    perm[1] = jnp.where(row_id == along, 1.0, 0.0).astype(BF16)

    hs_tx[...] = jnp.zeros_like(hs_tx)
    etx[...] = jnp.zeros_like(etx)
    tap[...] = jnp.zeros_like(tap)

    ins[0].wait()
    gate = lg_ref[...]
    high = gate.astype(BF16).astype(F32)
    rest = gate - high
    mid_ = rest.astype(BF16).astype(F32)
    parts = (high, mid_, rest - mid_)
    stacked = jnp.concatenate(
        [x[:, :HALF] for x in parts] + [x[:, HALF:] for x in parts], axis=0
    ).astype(BF16)
    upto = jnp.where(row_id <= along, 1.0, 0.0).astype(BF16)
    sums_ = dot_nn(stacked, upto)
    run0 = sums_[0:8] + sums_[8:16] + sums_[16:24]
    run1 = sums_[24:32] + sums_[32:40] + sums_[40:48] + run0[:, HALF - 1 : HALF]
    run = jnp.concatenate([run0, run1], axis=1)
    run_t = run.T
    for h in range(heads):
        colb[h] = jnp.broadcast_to(run_t[:, h : h + 1], (GROUP, HD))
        rowb[h] = jnp.broadcast_to(run[h : h + 1, :], (8, GROUP))
        closb[h] = jnp.broadcast_to(run[h : h + 1, GROUP - 1 : GROUP], (8, HD))

    def spread(c, i, dst):
        ins[i].wait()
        for half in range(2):
            for k in range(0, width, chunk):
                cols = pl.ds(k, chunk)
                dst(half)[:, cols] = dot_nn(perm[0], ext[c, pl.ds(half * HALF, HALF), cols])

    def gather(src):
        return dot_nn(perm[1], src).astype(BF16)

    first = lax.broadcasted_iota(jnp.int32, (8, width), 0) == 0
    last = lax.broadcasted_iota(jnp.int32, (8, width), 0) == 7

    def lead(c, half):
        if half == 0:
            edge_rows = hal[c].astype(F32)
        for j in range(1, TAPS):
            r = LEAD + HALF - 8 * j
            if half == 0:
                before = edge_rows[EDGE - j : EDGE - j + 1]
            else:
                before = xf[c, 0, pl.ds(r + 7, 1), :]
            xf[c, half, pl.ds(LEAD - 8 * j, 8), :] = jnp.where(
                first, jnp.broadcast_to(before, (8, width)), pltpu.roll(xf[c, half, pl.ds(r, 8), :], 1, 0)
            )

    def half_of(c):
        return lambda half: xf.at[c, half, pl.ds(LEAD, HALF), :]

    def conv(c, h, half, lo, count):
        cols = cols_of(h)
        y = w_ref[c, 0:1, cols] * xf[c, half, pl.ds(LEAD + lo, count), cols]
        for j in range(1, TAPS):
            y = y + w_ref[c, j : j + 1, cols] * xf[c, half, pl.ds(LEAD + lo - 8 * j, count), cols]
        convs[c][pl.ds(half * HALF + lo, count), cols] = y.astype(BF16)

    def shrink_of(h):
        return jnp.exp(closb[h][0:1, :] - colb[h])

    def halo(c):
        return ctx_copy(
            (q_hbm, k_hbm, v_hbm)[c].at[pl.ds(GROUP - EDGE, EDGE), :], hal.at[c],
            ha_s.at[c], ha_r.at[c], lax.rem(me + 1, n),
        )

    clos_pair = ctx_copy(closb, closp, cp_s.at[0], cp_r.at[0], partner)
    pl.semaphore_wait(barrier, chips - 1 + 2 + m - 1)

    @pl.when(me < n - 1)
    def _():
        for c in (1, 2, 0):
            halo(c).start()

    clos_pair.start()

    @pl.when(me == 0)
    def _():
        hal[...] = jnp.zeros_like(hal)

    spread(1, 1, half_of(1))
    spread(2, 2, half_of(2))
    ins[3].wait()
    lead(1, 1)
    lead(2, 1)

    def local_state(h, i):
        cols = cols_of(h)
        for c in (1, 2):
            conv(c, h, 0, FIX, HALF - FIX)
            conv(c, h, 1, 0, HALF)
        ks = (kc[FIX:, cols].astype(F32) * shrink_of(h)[FIX:]).astype(BF16)
        local[h] = dot_tn(ks, vc[FIX:, cols])

    group(theirs, local_state)
    group(mine, local_state)

    @pl.when(me > 0)
    def _():
        halo(1).wait_recv()
        halo(2).wait_recv()

    lead(1, 0)
    lead(2, 0)

    def whole_state(h):
        cols = cols_of(h)
        for c in (1, 2):
            conv(c, h, 0, 0, FIX)
        shrink = jnp.exp(closb[h][0:1, :] - colb[h, :FIX])
        ks = (kc[:FIX, cols].astype(F32) * shrink).astype(BF16)
        return local[h] + dot_tn(ks, vc[:FIX, cols])

    def their_state(h, i):
        fx_t[i] = whole_state(h).astype(BF16)

    group(theirs, their_state)
    fx = ctx_copy(fx_t, fx_r, fx_s.at[0], fx_q.at[0], partner)
    fx.start()

    def my_state(h, i):
        local[h] = whole_state(h)

    group(mine, my_state)

    def clos_copy(p, source):
        return ctx_copy(
            closc.at[p // per], closr.at[source], cl_s.at[p], cl_r.at[source], 2 * p + core
        )

    clos_pair.wait_recv()
    for i in range(hc):
        closc[i] = closb[mine + i] + closp[mine + i]
    peers(owners, lambda p: clos_copy(p, chip).start())

    def own_clos():
        closr[chip] = closc[chip // per]

    owning(own_clos)

    def decay(h, c):
        col = colb[h]
        row = rowb[h][0:1, :]
        top = jnp.concatenate([col[:HALF]] * 2, axis=1)
        low = jnp.concatenate([col[HALF:]] * 2, axis=1)
        keep = times((HALF, HALF), 0) >= times((HALF, HALF), 1)
        w0[h] = jnp.where(keep, jnp.exp(jnp.minimum(top - row[:, :HALF], 0.0)), 0.0)
        w1[h, :, :HALF] = jnp.exp(jnp.minimum(low - row[:, :HALF], 0.0))
        w1[h, :, HALF:] = jnp.where(keep, jnp.exp(jnp.minimum(low - row[:, HALF:], 0.0)), 0.0)

    def slice_copy(src, dst, ss, rs, o, source):
        return ctx_copy(src.at[o], dst.at[source], ss.at[o], rs.at[source], 2 * o + core)

    def hand_out(leads, theirs_r, src, dst, ss, rs):
        for i in range(hc):
            a = jnp.where(leads, jnp.exp(closp[mine + i][0:1, :]), 1.0)
            b = jnp.where(leads, 1.0, jnp.exp(closb[mine + i][0:1, :]))
            both = (a * local[mine + i] + b * theirs_r[i].astype(F32)).astype(BF16)
            for k in range(per):
                src[i * per + k] = both[k * R : (k + 1) * R]
        peers(owners, lambda o: slice_copy(src, dst, ss, rs, o, chip).start())

        def keep():
            dst[chip] = src[chip]

        owning(keep)

    def scan_slices(backwards, src, ss, got, rs, out, res, ss2, rs2):
        def take():
            peers(chips, lambda s: slice_copy(src, got, ss, rs, 0, s).wait_recv())

            def step(i, state):
                b = chips - 1 - i if backwards else i
                out[b] = state.astype(BF16)
                return jnp.exp(closr[b][0:1, :]) * state + got[b].astype(F32)

            state = jnp.zeros((R, HD), F32)
            if chips <= UNROLL:
                for i in range(chips):
                    state = step(i, state)
            else:
                lax.fori_loop(0, chips, step, state)
            peers(chips, lambda p: result_copy(out, res, ss2, rs2, p, chip).start())
            res[chip] = out[chip]

        owning(take)

    def result_copy(out, res, ss2, rs2, p, source):
        return ctx_copy(
            out.at[p], res.at[source], ss2.at[p], rs2.at[source], 2 * p + core
        )

    def pass_on(leads, theirs_r, out, res, ss2, rs2, ptx, pin, ps, pr):
        peers(owners, lambda o: result_copy(out, res, ss2, rs2, 0, o).wait_recv())
        for i in range(hc):
            p = res[pl.ds(i * per, per)].reshape(HD, HD).astype(F32)
            follow = jnp.exp(closb[mine + i][0:1, :]) * p + local[mine + i]
            ptx[i] = jnp.where(leads, follow, p).astype(BF16)
        copy = ctx_copy(ptx, pin.at[pl.ds(mine, hc)], ps.at[0], pr.at[0], partner)
        copy.start()
        for i in range(hc):
            p = res[pl.ds(i * per, per)].reshape(HD, HD).astype(F32)
            follow = jnp.exp(closp[mine + i][0:1, :]) * p + theirs_r[i].astype(F32)
            pin[mine + i] = jnp.where(leads, p, follow).astype(BF16)
        return ctx_copy(ptx, pin.at[pl.ds(theirs, hc)], ps.at[0], pr.at[0], partner)

    ahead = core == 0
    over(0, heads, decay)
    fx.wait_recv()
    hand_out(ahead, fx_r, fs, fr, f1_s, f1_r)

    spread(0, 4, half_of(0))

    @pl.when(me > 0)
    def _():
        halo(0).wait_recv()

    lead(0, 1)
    lead(0, 0)

    def inner(h, c):
        cols = cols_of(h)
        conv(0, h, 0, 0, HALF)
        conv(0, h, 1, 0, HALF)
        q0, q1 = qc[:HALF, cols], qc[HALF:, cols]
        a0 = (dot_nt(q0, kc[:HALF, cols]) * w0[h]).astype(BF16)
        a1 = (dot_nt(q1, kc[:, cols]) * w1[h]).astype(BF16)
        p0[h] = a0
        p1[h] = a1
        att[:HALF, cols] = dot_nn(a0, vc[:HALF, cols])
        att[HALF:, cols] = dot_nn(a1, vc[:, cols])

    mid = max(heads * 3 // 4, 1)
    over(0, mid, inner)

    def clos_in():
        peers(chips, lambda s: clos_copy(chip, s).wait_recv())

    owning(clos_in)
    scan_slices(False, fs, f1_s, fr, f1_r, fo, fi, f2_s, f2_r)
    over(mid, heads, inner)
    spread(3, 5, lambda half: gf.at[pl.ds(half * HALF, HALF), :])
    ins[6].wait()
    fp_in = pass_on(ahead, fx_r, fo, fi, f2_s, f2_r, fp, fin, fp_s, fp_r)

    accs[...] = jnp.zeros_like(accs)
    acci[...] = jnp.zeros_like(acci)

    def outer(h, c):
        cols = cols_of(h)
        a = att[:, cols] + dot_nn(qc[:, cols], fin[h]) * jnp.exp(colb[h])
        att[:, cols] = a
        accs[...] += a * a
        acci[...] += gf[:, cols] * gain_ref[0:1, cols] * a

    group(mine, outer)
    fp_in.wait_recv()
    group(theirs, outer)
    hs_tx[0:1, :] = jnp.sum(accs[...].T, axis=0, keepdims=True)
    hs_tx[1:2, :] = jnp.sum(acci[...].T, axis=0, keepdims=True)

    def sums_copy(p, source):
        return head_copy(hs_tx, hs_rx.at[source], hs_s.at[p], hs_r.at[source], p)

    for d in range(1, m):
        sums_copy(lax.rem(hme + d, m), hme).start()
    hs_rx[hme] = hs_tx[...]
    for d in range(1, m):
        sums_copy(hme, lax.rem(hme + d, m)).wait_recv()
    sums = hs_rx[0]
    for d in range(1, m):
        sums = sums + hs_rx[d]
    inverse = lax.rsqrt(sums[0:1, :] / total + EPS)
    coef = inverse * inverse * (sums[1:2, :] / total)
    both = jnp.concatenate([inverse, coef, jnp.zeros((6, GROUP), F32)], axis=0).T
    invb[...] = jnp.broadcast_to(both[:, 0:1], (GROUP, HD))
    coefb[...] = jnp.broadcast_to(both[:, 1:2], (GROUP, HD))

    def norm(h, c):
        cols = cols_of(h)
        a = att[:, cols]
        inv = invb[...]
        normed = a * inv
        gain = gain_ref[0:1, cols]
        gw = gf[:, cols]
        mixb[:, cols] = (normed * gain).astype(BF16)
        tap[0, 4:5, cols] = jnp.sum(gw * normed, axis=0, keepdims=True)
        o = (inv * (gw * gain - a * coefb[...])).astype(BF16)
        og[:, cols] = o
        qs = (qc[:, cols].astype(F32) * jnp.exp(colb[h])).astype(BF16)
        return dot_tn(qs, o)

    def their_norm(h, i):
        bx_t[i] = norm(h, i).astype(BF16)

    def my_norm(h, i):
        local[h] = norm(h, i)

    behind = core == 1
    group(theirs, their_norm)
    bx = ctx_copy(bx_t, bx_r, bx_s.at[0], bx_q.at[0], partner)
    bx.start()
    group(mine, my_norm)
    bx.wait_recv()
    hand_out(behind, bx_r, bs, br, b1_s, b1_r)

    def back(h, c):
        cols = cols_of(h)
        o0, o1 = og[:HALF, cols], og[HALF:, cols]
        s0 = (dot_nt(o0, vc[:HALF, cols]) * w0[h]).astype(BF16)
        s1 = (dot_nt(o1, vc[:, cols]) * w1[h]).astype(BF16)
        through = dot_nt(og[:, cols], fin[h]) * jnp.exp(colb[h])
        cg[0, 0, :HALF, cols] = dot_nn(s0, kc[:HALF, cols]) + through[:HALF]
        cg[0, 1, :HALF, cols] = dot_nn(s1, kc[:, cols]) + through[HALF:]
        kk = dot_tn(s1, qc[HALF:, cols])
        cg[1, 0, :HALF, cols] = kk[:HALF] + dot_tn(s0, qc[:HALF, cols])
        cg[1, 1, :HALF, cols] = kk[HALF:]
        vv = dot_tn(p1[h], o1)
        cg[2, 0, :HALF, cols] = vv[:HALF] + dot_tn(p0[h], o0)
        cg[2, 1, :HALF, cols] = vv[HALF:]

    over(0, mid, back)
    scan_slices(True, bs, b1_s, br, b1_r, bo, bi, b2_s, b2_r)
    over(mid, heads, back)

    def edge(c):
        return ctx_copy(
            etx.at[c], erx.at[c], eh_s.at[c], eh_r.at[c], lax.rem(me + n - 1, n)
        )

    def send_edge(c):
        for j in range(TAPS - 1):
            etx[c, j : j + 1, :] = cg[c, 0, pl.ds(8 * j, 1), :]

        @pl.when(me > 0)
        def _():
            edge(c).start()

    @pl.when(me == n - 1)
    def _():
        erx[...] = jnp.zeros_like(erx)

    send_edge(0)

    def taps(c, h):
        cols = cols_of(h)
        for j in range(TAPS):
            part = 0.0
            for half in range(2):
                part = part + jnp.sum(
                    cg[c, half, pl.ds(0, HALF), cols]
                    * xf[c, half, pl.ds(LEAD - 8 * j, HALF), cols],
                    axis=0, keepdims=True,
                )
            r = j + TAPS * (c == 2)
            tap[int(c > 0), r : r + 1, cols] = part

    def q_taps(h, c):
        taps(0, h)

    over(0, heads, q_taps)

    def tap_pair(s):
        return ctx_copy(tap.at[s], tapp.at[s], tp_s.at[s], tp_r.at[s], partner)

    def tap_copy(s, p, source):
        return ctx_copy(
            tapb.at[s], tapr.at[s, source], t_s.at[s, p], t_r.at[s, source], 2 * p + core
        )

    def spread_taps(s):
        tap_pair(s).wait_recv()
        both_ = tap[s] + tapp[s]
        tapb[s] = jnp.concatenate(
            [both_[:, : width // 2], both_[:, width // 2 :]], axis=0
        ).astype(BF16)
        peers(chips, lambda p: tap_copy(s, p, chip).start())

    tap_pair(0).start()
    for half in range(2):
        for k in range(0, width, chunk):
            cols = pl.ds(k, chunk)
            rows = pl.ds(half * HALF, HALF)
            mix_ref[rows, cols] = gather(mixb[rows, cols])
    spread_taps(0)
    bp_in = pass_on(behind, bx_r, bo, bi, b2_s, b2_r, bp, bin_, bp_s, bp_r)

    def late(h, c):
        cols = cols_of(h)
        state = bin_[h]
        sh = shrink_of(h)
        for i, add in ((1, dot_nt(vc[:, cols], state) * sh), (2, dot_nn(kc[:, cols], state) * sh)):
            cg[i, 0, :HALF, cols] += add[:HALF]
            cg[i, 1, :HALF, cols] += add[HALF:]
        taps(1, h)
        taps(2, h)

    group(mine, late)
    bp_in.wait_recv()
    group(theirs, late)
    tap_pair(1).start()
    send_edge(1)
    send_edge(2)

    def edge_in(c):
        @pl.when(me < n - 1)
        def _():
            edge(c).wait_recv()

    def unconv(c):
        edge_in(c)
        for j in range(TAPS - 1):
            after = jnp.broadcast_to(erx[c, j : j + 1, :], (8, width))
            for half in (1, 0):
                moved = pltpu.roll(cg[c, half, pl.ds(8 * j, 8), :], 7, 0)
                cg[c, half, pl.ds(HALF + 8 * j, 8), :] = jnp.where(last, after, moved)
                after = moved
        for half in range(2):
            for k in range(0, width, chunk):
                cols = pl.ds(k, chunk)
                y = w_ref[c, 0:1, cols] * cg[c, half, pl.ds(0, HALF), cols]
                for j in range(1, TAPS):
                    y = y + w_ref[c, j : j + 1, cols] * cg[c, half, pl.ds(8 * j, HALF), cols]
                outs[c][pl.ds(half * HALF, HALF), cols] = gather(y.astype(BF16))

    outs = (qg_ref, kg_ref, vg_ref)
    spread_taps(1)
    unconv(0)
    unconv(1)
    unconv(2)

    def sum_taps(s):
        tapr[s, chip] = tapb[s]
        peers(chips, lambda p: tap_copy(s, 0, p).wait_recv())
        wide = tapr[s, 0].astype(F32)
        if chips <= UNROLL:
            for p in range(1, chips):
                wide = wide + tapr[s, p].astype(F32)
        else:
            wide = lax.fori_loop(1, chips, lambda p, a: a + tapr[s, p].astype(F32), wide)
        return jnp.concatenate([wide[:8], wide[8:]], axis=1)

    q_sums = sum_taps(0)
    cgrad_ref[0] = q_sums[0:4]
    ggrad_ref[...] = q_sums[4:5]
    kv_sums = sum_taps(1)
    cgrad_ref[1] = kv_sums[0:4]
    cgrad_ref[2] = kv_sums[4:8]

    @pl.when(me < n - 1)
    def _():
        for c in range(3):
            halo(c).wait_send()

    @pl.when(me > 0)
    def _():
        for c in range(3):
            edge(c).wait_send()

    clos_pair.wait_send()
    fx.wait_send()
    bx.wait_send()
    fp_in.wait_send()
    bp_in.wait_send()

    def sent_to_owner(o):
        clos_copy(o, chip).wait_send()
        slice_copy(fs, fr, f1_s, f1_r, o, chip).wait_send()
        slice_copy(bs, br, b1_s, b1_r, o, chip).wait_send()

    peers(owners, sent_to_owner)

    def sent_states():
        def one(p):
            result_copy(fo, fi, f2_s, f2_r, p, chip).wait_send()
            result_copy(bo, bi, b2_s, b2_r, p, chip).wait_send()

        peers(chips, one)

    owning(sent_states)
    for d in range(1, m):
        sums_copy(lax.rem(hme + d, m), hme).wait_send()
    for s in range(2):
        tap_pair(s).wait_send()
        peers(chips, lambda p: tap_copy(s, p, chip).wait_send())


def hand_on(*refs):
    count = (len(refs) - 1) // 2
    put = refs[-1]
    moves = [
        pltpu.make_async_copy(refs[i], refs[count + i], put.at[i]) for i in range(count)
    ]
    for cp in moves:
        cp.start()
    for cp in moves:
        cp.wait()


def body(n, m, query_rows, key_rows, value_rows, log_gate, conv_weight, norm_gain, mixed_grad):
    tok_here, width = query_rows.shape
    assert tok_here == GROUP
    heads = width // HD
    chips = n // 2
    hc = heads // 2
    owners = min(chips, hc * HD // 16)
    R = hc * HD // owners
    if heads < 8:
        log_gate = jnp.pad(log_gate, ((0, 8 - heads), (0, 0)))
    any_ = pl.BlockSpec(memory_space=pl.ANY)
    vm = pl.BlockSpec(memory_space=pltpu.VMEM)
    V = pltpu.VMEM
    S = pltpu.SemaphoreType.DMA
    hbm = pl.BlockSpec(memory_space=pltpu.HBM)
    result = pl.pallas_call(
        functools.partial(kernel, n, m, heads, owners),
        out_shape=(
            V((GROUP, width), BF16), V((GROUP, width), BF16),
            V((GROUP, width), BF16), V((GROUP, width), BF16),
            V((3, TAPS, width), F32), V((1, width), F32),
        ),
        in_specs=[hbm] * 7,
        out_specs=(vm,) * 6,
        scratch_shapes=[
            V((4, GROUP, width), BF16),
            V((3, EDGE, width), BF16),
            V((8, GROUP), F32),
            V((3, TAPS, width), F32),
            V((1, width), F32),
            V((2, HALF, HALF), BF16),
            V((3, 2, LEAD + HALF, width), F32),
            V((GROUP, width), BF16),
            V((GROUP, width), BF16),
            V((GROUP, width), BF16),
            V((GROUP, width), F32),
            V((GROUP, width), F32),
            V((GROUP, width), BF16),
            V((GROUP, width), BF16),
            V((3, 2, HALF + LEAD, width), F32),
            V((3, 8, width), F32),
            V((3, 8, width), F32),
            V((heads, HALF, HALF), F32),
            V((heads, HALF, GROUP), F32),
            V((heads, HALF, HALF), BF16),
            V((heads, HALF, GROUP), BF16),
            V((heads, GROUP, HD), F32),
            V((heads, 8, GROUP), F32),
            V((heads, 8, HD), F32),
            V((heads, 8, HD), F32),
            V((hc, 8, HD), F32),
            V((chips, 8, HD), F32),
            V((heads, HD, HD), F32),
            V((hc, HD, HD), BF16),
            V((hc, HD, HD), BF16),
            V((owners, R, HD), BF16),
            V((chips, R, HD), BF16),
            V((chips, R, HD), BF16),
            V((owners, R, HD), BF16),
            V((hc, HD, HD), BF16),
            V((heads, HD, HD), BF16),
            V((hc, HD, HD), BF16),
            V((hc, HD, HD), BF16),
            V((owners, R, HD), BF16),
            V((chips, R, HD), BF16),
            V((chips, R, HD), BF16),
            V((owners, R, HD), BF16),
            V((hc, HD, HD), BF16),
            V((heads, HD, HD), BF16),
            V((GROUP, HD), F32),
            V((GROUP, HD), F32),
            V((GROUP, HD), F32),
            V((GROUP, HD), F32),
            V((8, GROUP), F32),
            V((m, 8, GROUP), F32),
            V((2, 8, width), F32),
            V((2, 8, width), F32),
            V((2, 16, width // 2), BF16),
            V((2, chips, 16, width // 2), BF16),
            S((7,)), S((3,)), S((3,)), S((1,)), S((1,)), S((chips,)), S((chips,)),
            S((1,)), S((1,)), S((chips,)), S((chips,)), S((chips,)), S((chips,)), S((1,)), S((1,)),
            S((1,)), S((1,)), S((chips,)), S((chips,)), S((chips,)), S((chips,)), S((1,)), S((1,)),
            S((m,)), S((m,)), S((3,)), S((3,)), S((2,)), S((2,)), S((2, chips)), S((2, chips)),
        ],
        compiler_params=pltpu.CompilerParams(
            collective_id=0, has_side_effects=True, vmem_limit_bytes=52 * 1024 * 1024
        ),
    )(
        query_rows, key_rows, value_rows, mixed_grad,
        log_gate, conv_weight, norm_gain.reshape(1, width),
    )
    result = pl.pallas_call(
        hand_on,
        out_shape=tuple(jax.ShapeDtypeStruct(r.shape, r.dtype) for r in result),
        in_specs=[any_] * 6,
        out_specs=(any_,) * 6,
        scratch_shapes=[S((6,))],
        compiler_params=pltpu.CompilerParams(vmem_limit_bytes=4 * 1024 * 1024),
    )(*result)
    return (*result[:5], result[5].reshape(width))


def solution(mesh):
    n, m = mesh.shape["ctx"], mesh.shape["head"]
    rows = P("ctx", "head")
    return jax.shard_map(
        functools.partial(body, n, m),
        mesh=mesh,
        in_specs=(rows, rows, rows, P("head", "ctx"), P(None, None, "head"), P("head"), rows),
        out_specs=(rows, rows, rows, rows, P(None, None, "head"), P("head")),
        check_vma=False,
    )
```

```python
import functools

import jax
import jax.numpy as jnp
from jax import lax
from jax.experimental import pallas as pl
from jax.experimental.pallas import tpu as pltpu
from jax.sharding import PartitionSpec as P

HD = 128
TAPS = 4
GROUP = 512
HALF = GROUP // 2
UNROLL = 8
SEG = HALF // 8
LEAD = 8 * (TAPS - 1)
EDGE = 16
FIX = 32
PIECES = 1
EPS = 1e-05
MESH = pl.DeviceIdType.MESH
F32 = jnp.float32
BF16 = jnp.bfloat16


def dot_nn(a, b):
    return lax.dot_general(a, b, (((1,), (0,)), ((), ())), preferred_element_type=F32)


def dot_nt(a, b):
    return lax.dot_general(a, b, (((1,), (1,)), ((), ())), preferred_element_type=F32)


def dot_tn(a, b):
    return lax.dot_general(a, b, (((0,), (0,)), ((), ())), preferred_element_type=F32)


def times(shape, axis):
    p = lax.broadcasted_iota(jnp.int32, shape, axis)
    return (p & 7) * SEG + (p >> 3)


def kernel(
    n, m, heads, owners,
    q_hbm, k_hbm, v_hbm, g_hbm, lg_hbm, w_hbm, gain_hbm,
    mix_ref, qg_ref, kg_ref, vg_ref, cgrad_ref, ggrad_ref,
    ext, hal, lg_ref, w_ref, gain_ref, perm,
    xf, qc, kc, vc, qsb, gf, ggf, att, og, cg, etx, erx,
    w0, w1, p0, p1, colb, grow, shr, rowb, closb, closp, closc, closr,
    x4, wown, wtx, wrx, tapl,
    local, fx_t, fx_r, fs, fr, fo, fi, fp, fin,
    bx_t, bx_r, bs, br, bo, bi, bp, bin_,
    accs, acci, invb, coefb, hs_tx, hs_rx,
    tap, tapp, tapb, tapr,
    loc, ha_s, ha_r, cp_s, cp_r, cl_s, cl_r,
    fx_s, fx_q, f1_s, f1_r, f2_s, f2_r, fp_s, fp_r,
    bx_s, bx_q, b1_s, b1_r, b2_s, b2_r, bp_s, bp_r,
    hs_s, hs_r, eh_s, eh_r, tp_s, tp_r, t_s, t_r, wp_s, wp_r,
):
    me = lax.axis_index("ctx")
    hme = lax.axis_index("head")
    chips = n // 2
    chip = me // 2
    core = lax.rem(me, 2)
    partner = me + 1 - 2 * core
    hc = heads // 2
    mine = core * hc
    theirs = hc - mine
    per = owners // hc
    R = HD // per
    width = heads * HD
    total = width * m
    convs = (qc, kc, vc)
    chunk = min(2 * HD, width)

    def ctx_copy(src, dst, ss, rs, p):
        return pltpu.make_async_remote_copy(
            src_ref=src, dst_ref=dst, send_sem=ss, recv_sem=rs,
            device_id={"ctx": p}, device_id_type=MESH,
        )

    def head_copy(src, dst, ss, rs, p):
        return pltpu.make_async_remote_copy(
            src_ref=src, dst_ref=dst, send_sem=ss, recv_sem=rs,
            device_id={"head": p}, device_id_type=MESH,
        )

    def peers(count, fn):
        def one(d, c):
            p = lax.rem(chip + d, chips)
            if count == chips:
                fn(p)
            else:
                pl.when(p < count)(lambda: fn(p))
            return c

        lax.fori_loop(1, chips, one, 0)

    def everyone(fn):
        def one(d, c):
            fn(lax.rem(me + d, n))
            return c

        lax.fori_loop(1, n, one, 0)

    single = owners == chips

    def slot(sem, i):
        return sem.at[0] if single else sem.at[i]

    def bulk(ref, count, sem):
        rows = ref.at[pl.ds(0, count)]
        return ctx_copy(rows, rows, sem.at[0], sem.at[0], partner)

    def arrived(ref, sem, count, one):
        if single:
            bulk(ref, chips - 1, sem).wait_recv()
        else:
            peers(count, one)

    def sent(ref, sem):
        bulk(ref, chips - 1, sem).wait_send()

    def owning(fn):
        if owners == chips:
            fn()
        else:
            pl.when(chip < owners)(fn)

    def cols_of(h):
        if isinstance(h, int):
            return pl.ds(h * HD, HD)
        return pl.ds(pl.multiple_of(h * HD, HD), HD)

    def over(lo, hi, fn):
        for h in range(lo, hi):
            fn(h, 0)

    def group(first, fn):
        for i in range(hc):
            fn(first + i, i)

    ins = [
        pltpu.make_async_copy(src, dst, loc.at[i])
        for i, (src, dst) in enumerate((
            (lg_hbm, lg_ref), (k_hbm, ext.at[1]), (v_hbm, ext.at[2]),
            (w_hbm, w_ref), (q_hbm, ext.at[0]), (g_hbm, ext.at[3]), (gain_hbm, gain_ref),
        ))
    ]
    for cp in ins:
        cp.start()

    barrier = pltpu.get_barrier_semaphore()

    def greet(p):
        pl.semaphore_signal(barrier, inc=1, device_id={"ctx": p}, device_id_type=MESH)

    everyone(greet)
    for d in range(1, m):
        pl.semaphore_signal(
            barrier, inc=1, device_id={"head": lax.rem(hme + d, m)}, device_id_type=MESH
        )

    at = times((HALF, HALF), 0)
    along = times((HALF, HALF), 1)
    row_id = lax.broadcasted_iota(jnp.int32, (HALF, HALF), 0)
    lane_id = lax.broadcasted_iota(jnp.int32, (HALF, HALF), 1)
    perm[0] = jnp.where(at == lane_id, 1.0, 0.0).astype(BF16)
    perm[1] = jnp.where(row_id == along, 1.0, 0.0).astype(BF16)

    etx[...] = jnp.zeros_like(etx)
    tap[...] = jnp.zeros_like(tap)

    ins[0].wait()
    gate = lg_ref[...]
    high = gate.astype(BF16).astype(F32)
    rest = gate - high
    mid_ = rest.astype(BF16).astype(F32)
    parts = (high, mid_, rest - mid_)
    stacked = jnp.concatenate(
        [x[:, :HALF] for x in parts] + [x[:, HALF:] for x in parts], axis=0
    ).astype(BF16)
    upto = jnp.where(row_id <= along, 1.0, 0.0).astype(BF16)
    sums_ = dot_nn(stacked, upto)
    run0 = sums_[0:8] + sums_[8:16] + sums_[16:24]
    run1 = sums_[24:32] + sums_[32:40] + sums_[40:48] + run0[:, HALF - 1 : HALF]
    run = jnp.concatenate([run0, run1], axis=1)
    run_t = run.T
    for h in range(heads):
        colb[h] = jnp.broadcast_to(run_t[:, h : h + 1], (GROUP, HD))
        rowb[h] = jnp.broadcast_to(run[h : h + 1, :], (8, GROUP))
        closb[h] = jnp.broadcast_to(run[h : h + 1, GROUP - 1 : GROUP], (8, HD))

    def spread(c, i, dst):
        ins[i].wait()
        for half in range(2):
            for k in range(0, width, chunk):
                cols = pl.ds(k, chunk)
                dst(half)[:, cols] = dot_nn(perm[0], ext[c, pl.ds(half * HALF, HALF), cols])

    def gather(src):
        return dot_nn(perm[1], src).astype(BF16)

    first = lax.broadcasted_iota(jnp.int32, (8, width), 0) == 0
    last = lax.broadcasted_iota(jnp.int32, (8, width), 0) == 7

    def lead(c, half):
        if half == 0:
            edge_rows = hal[c].astype(F32)
        for j in range(1, TAPS):
            r = LEAD + HALF - 8 * j
            if half == 0:
                before = edge_rows[EDGE - j : EDGE - j + 1]
            else:
                before = xf[c, 0, pl.ds(r + 7, 1), :]
            xf[c, half, pl.ds(LEAD - 8 * j, 8), :] = jnp.where(
                first, jnp.broadcast_to(before, (8, width)), pltpu.roll(xf[c, half, pl.ds(r, 8), :], 1, 0)
            )

    def half_of(c):
        return lambda half: xf.at[c, half, pl.ds(LEAD, HALF), :]

    def conv(c, h, half, lo, count):
        cols = cols_of(h)
        end = lo + count
        while lo < end:
            now = min(HD - lo % HD, end - lo)
            rows = xf[c, half, pl.ds(lo, LEAD + now), cols]
            y = w_ref[c, 0:1, cols] * rows[LEAD:]
            for j in range(1, TAPS):
                y = y + w_ref[c, j : j + 1, cols] * rows[LEAD - 8 * j : LEAD - 8 * j + now]
            convs[c][pl.ds(half * HALF + lo, now), cols] = y.astype(BF16)
            lo += now

    def halo(c):
        return ctx_copy(
            (q_hbm, k_hbm, v_hbm)[c].at[pl.ds(GROUP - EDGE, EDGE), :], hal.at[c],
            ha_s.at[c], ha_r.at[c], lax.rem(me + 1, n),
        )

    clos_pair = ctx_copy(closb, closp, cp_s.at[0], cp_r.at[0], partner)
    pl.semaphore_wait(barrier, n - 1 + m - 1)

    @pl.when(me < n - 1)
    def _():
        for c in (1, 2, 0):
            halo(c).start()

    clos_pair.start()

    @pl.when(me == 0)
    def _():
        hal[...] = jnp.zeros_like(hal)

    spread(1, 1, half_of(1))
    spread(2, 2, half_of(2))
    ins[3].wait()
    lead(1, 1)
    lead(2, 1)

    def local_state(h, i):
        cols = cols_of(h)
        for c in (1, 2):
            conv(c, h, 0, FIX, HALF - FIX)
            conv(c, h, 1, 0, HALF)
        shr[h] = jnp.exp(closb[h][0:1, :] - colb[h])
        ks = (kc[FIX:, cols].astype(F32) * shr[h, FIX:]).astype(BF16)
        local[h] = dot_tn(ks, vc[FIX:, cols])

    group(theirs, local_state)
    group(mine, local_state)

    @pl.when(me > 0)
    def _():
        halo(1).wait_recv()
        halo(2).wait_recv()

    lead(1, 0)
    lead(2, 0)

    def whole_state(h):
        cols = cols_of(h)
        for c in (1, 2):
            conv(c, h, 0, 0, FIX)
        ks = (kc[:FIX, cols].astype(F32) * shr[h, :FIX]).astype(BF16)
        return local[h] + dot_tn(ks, vc[:FIX, cols])

    def their_state(h, i):
        fx_t[i] = whole_state(h).astype(BF16)

    group(theirs, their_state)
    fx = ctx_copy(fx_t, fx_r, fx_s.at[0], fx_q.at[0], partner)
    fx.start()

    def my_state(h, i):
        local[h] = whole_state(h)

    group(mine, my_state)

    def clos_copy(p, source):
        return ctx_copy(
            closc.at[p // per], closr.at[source], slot(cl_s, p), slot(cl_r, source), 2 * p + core
        )

    clos_pair.wait_recv()
    for i in range(hc):
        closc[i] = closb[mine + i] + closp[mine + i]
    peers(owners, lambda p: clos_copy(p, chip).start())

    def own_clos():
        closr[chip] = closc[chip // per]

    owning(own_clos)

    def decay(h, c):
        col = colb[h]
        grow[h] = jnp.exp(col)
        row = rowb[h][0:1, :]
        top = jnp.concatenate([col[:HALF]] * 2, axis=1)
        low = jnp.concatenate([col[HALF:]] * 2, axis=1)
        keep = times((HALF, HALF), 0) >= times((HALF, HALF), 1)
        w0[h] = jnp.where(keep, jnp.exp(jnp.minimum(top - row[:, :HALF], 0.0)), 0.0)
        w1[h, :, :HALF] = jnp.exp(jnp.minimum(low - row[:, :HALF], 0.0))
        w1[h, :, HALF:] = jnp.where(keep, jnp.exp(jnp.minimum(low - row[:, HALF:], 0.0)), 0.0)

    def slice_copy(src, dst, ss, rs, o, source):
        return ctx_copy(src.at[o], dst.at[source], slot(ss, o), slot(rs, source), 2 * o + core)

    def hand_out(leads, theirs_r, src, dst, ss, rs):
        for i in range(hc):
            a = jnp.where(leads, jnp.exp(closp[mine + i][0:1, :]), 1.0)
            b = jnp.where(leads, 1.0, jnp.exp(closb[mine + i][0:1, :]))
            both = (a * local[mine + i] + b * theirs_r[i].astype(F32)).astype(BF16)
            for k in range(per):
                src[i * per + k] = both[k * R : (k + 1) * R]
        peers(owners, lambda o: slice_copy(src, dst, ss, rs, o, chip).start())

        def keep():
            dst[chip] = src[chip]

        owning(keep)

    def scan_slices(backwards, src, ss, got, rs, out, res, ss2, rs2):
        def take():
            arrived(got, rs, chips, lambda s: slice_copy(src, got, ss, rs, 0, s).wait_recv())

            def step(i, state):
                b = chips - 1 - i if backwards else i
                out[b] = state.astype(BF16)
                return jnp.exp(closr[b][0:1, :]) * state + got[b].astype(F32)

            state = jnp.zeros((R, HD), F32)
            if chips <= UNROLL:
                for i in range(chips):
                    state = step(i, state)
            else:
                lax.fori_loop(0, chips, step, state)
            peers(chips, lambda p: result_copy(out, res, ss2, rs2, p, chip).start())
            res[chip] = out[chip]

        owning(take)

    def result_copy(out, res, ss2, rs2, p, source):
        return ctx_copy(
            out.at[p], res.at[source], slot(ss2, p), slot(rs2, source), 2 * p + core
        )

    def pass_on(leads, theirs_r, res, ptx, pin, ps, pr):
        for i in range(hc):
            p = res[pl.ds(i * per, per)].reshape(HD, HD).astype(F32)
            follow = jnp.exp(closb[mine + i][0:1, :]) * p + local[mine + i]
            ptx[i] = jnp.where(leads, follow, p).astype(BF16)
        copy = ctx_copy(ptx, pin.at[pl.ds(mine, hc)], ps.at[0], pr.at[0], partner)
        copy.start()
        for i in range(hc):
            p = res[pl.ds(i * per, per)].reshape(HD, HD).astype(F32)
            follow = jnp.exp(closp[mine + i][0:1, :]) * p + theirs_r[i].astype(F32)
            pin[mine + i] = jnp.where(leads, p, follow).astype(BF16)
        return ctx_copy(ptx, pin.at[pl.ds(theirs, hc)], ps.at[0], pr.at[0], partner)

    ahead = core == 0
    over(0, heads, decay)
    fx.wait_recv()
    hand_out(ahead, fx_r, fs, fr, f1_s, f1_r)

    spread(0, 4, half_of(0))

    @pl.when(me > 0)
    def _():
        halo(0).wait_recv()

    lead(0, 1)
    lead(0, 0)

    def inner(h, c):
        cols = cols_of(h)
        conv(0, h, 0, 0, HALF)
        conv(0, h, 1, 0, HALF)
        q0, q1 = qc[:HALF, cols], qc[HALF:, cols]
        a0 = (dot_nt(q0, kc[:HALF, cols]) * w0[h]).astype(BF16)
        a1 = (dot_nt(q1, kc[:, cols]) * w1[h]).astype(BF16)
        p0[h] = a0.T
        p1[h] = a1.T
        att[:HALF, cols] = dot_nn(a0, vc[:HALF, cols])
        att[HALF:, cols] = dot_nn(a1, vc[:, cols])
        qsb[h] = (qc[:, cols].astype(F32) * grow[h]).astype(BF16).T

    mid = max(heads * 3 // 4, 1)
    over(0, mid, inner)

    def clos_in():
        arrived(closr, cl_r, chips, lambda s: clos_copy(chip, s).wait_recv())

    owning(clos_in)
    scan_slices(False, fs, f1_s, fr, f1_r, fo, fi, f2_s, f2_r)
    over(mid, heads, inner)
    spread(3, 5, lambda half: gf.at[pl.ds(half * HALF, HALF), :])
    ins[6].wait()
    ggf[...] = gf[...] * gain_ref[...]

    def weigh(h):
        cols = cols_of(h)
        for i, src in ((1, vc), (2, kc)):
            for half in range(2):
                for lo in range(0, HALF, HD):
                    rows = xf[i, half, pl.ds(lo, LEAD + HD), cols]
                    for j in range(TAPS):
                        x4[i - 1, pl.ds(half * HALF + lo, HD), pl.ds(j * HD, HD)] = rows[
                            LEAD - 8 * j : LEAD - 8 * j + HD
                        ].astype(BF16)
            scaled = (src[:, cols].astype(F32) * shr[h]).astype(BF16)
            yield i - 1, dot_tn(scaled, x4[i - 1])

    def their_weights(h, i):
        for a, product in weigh(h):
            wtx[i, a] = product.astype(BF16)

    def my_weights(h, i):
        for a, product in weigh(h):
            wown[i, a] = product

    group(theirs, their_weights)
    w_pair = ctx_copy(wtx, wrx, wp_s.at[0], wp_r.at[0], partner)
    w_pair.start()
    arrived(fi, f2_r, owners, lambda o: result_copy(fo, fi, f2_s, f2_r, 0, o).wait_recv())
    fp_in = pass_on(ahead, fx_r, fi, fp, fin, fp_s, fp_r)


    def outer(h, c):
        cols = cols_of(h)
        a = att[:, cols] + dot_nn(qc[:, cols], fin[h]) * grow[h]
        att[:, cols] = a
        accs[...] += a * a
        acci[...] += ggf[:, cols] * a

    def outer_group(first_head, more):
        for lo in range(0, GROUP, HD):
            rows = pl.ds(lo, HD)
            square = accs[rows, :] if more else jnp.zeros((HD, HD), F32)
            inner_ = acci[rows, :] if more else jnp.zeros((HD, HD), F32)
            for i in range(hc):
                h = first_head + i
                cols = cols_of(h)
                a = att[rows, cols] + dot_nn(qc[rows, cols], fin[h]) * grow[h, rows]
                att[rows, cols] = a
                square = square + a * a
                inner_ = inner_ + ggf[rows, cols] * a
            accs[rows, :] = square
            acci[rows, :] = inner_

    outer_group(mine, False)
    fp_in.wait_recv()
    outer_group(theirs, True)
    for k, acc in ((0, accs), (4, acci)):
        row = jnp.sum(acc[...].T, axis=0, keepdims=True)
        for i in range(GROUP // HD):
            hs_tx[k + i : k + i + 1, :] = row[:, i * HD : (i + 1) * HD]

    def sums_copy(p, source):
        return head_copy(hs_tx, hs_rx.at[source], hs_s.at[p], hs_r.at[source], p)

    for d in range(1, m):
        sums_copy(lax.rem(hme + d, m), hme).start()
    hs_rx[hme] = hs_tx[...]
    group(mine, my_weights)
    for d in range(1, m):
        sums_copy(hme, lax.rem(hme + d, m)).wait_recv()
    sums = hs_rx[0]
    for d in range(1, m):
        sums = sums + hs_rx[d]
    inverse = lax.rsqrt(sums[0:4] / total + EPS)
    coef = inverse * inverse * (sums[4:8] / total)
    both = jnp.concatenate([inverse, coef], axis=0).T
    for i in range(GROUP // HD):
        rows = pl.ds(i * HD, HD)
        invb[rows, :] = jnp.broadcast_to(both[:, i : i + 1], (HD, HD))
        coefb[rows, :] = jnp.broadcast_to(both[:, 4 + i : 5 + i], (HD, HD))

    def norm(h, c):
        cols = cols_of(h)
        o = (invb[...] * (ggf[:, cols] - att[:, cols] * coefb[...])).astype(BF16)
        og[:, cols] = o
        return dot_nn(qsb[h], o)

    def their_norm(h, i):
        bx_t[i] = norm(h, i).astype(BF16)

    def my_norm(h, i):
        local[h] = norm(h, i)

    def mixing(k):
        cols = pl.ds(k, chunk)
        wide = jnp.concatenate([invb[...]] * (chunk // HD), axis=1)
        mixed = (att[:, cols] * wide * gain_ref[0:1, cols]).astype(BF16)
        for half in range(2):
            rows = pl.ds(half * HALF, HALF)
            mix_ref[rows, cols] = gather(mixed[half * HALF : (half + 1) * HALF])

    behind = core == 1
    group(theirs, their_norm)
    bx = ctx_copy(bx_t, bx_r, bx_s.at[0], bx_q.at[0], partner)
    bx.start()
    group(mine, my_norm)
    for k in range(0, width // 2, chunk):
        mixing(k)
    bx.wait_recv()
    hand_out(behind, bx_r, bs, br, b1_s, b1_r)

    def back(h, c):
        cols = cols_of(h)
        o0, o1 = og[:HALF, cols], og[HALF:, cols]
        s0 = (dot_nt(o0, vc[:HALF, cols]) * w0[h]).astype(BF16)
        s1 = (dot_nt(o1, vc[:, cols]) * w1[h]).astype(BF16)
        through = dot_nt(og[:, cols], fin[h]) * grow[h]
        cg[0, 0, :HALF, cols] = dot_nn(s0, kc[:HALF, cols]) + through[:HALF]
        cg[0, 1, :HALF, cols] = dot_nn(s1, kc[:, cols]) + through[HALF:]
        kk = dot_tn(s1, qc[HALF:, cols])
        cg[1, 0, :HALF, cols] = kk[:HALF] + dot_tn(s0, qc[:HALF, cols])
        cg[1, 1, :HALF, cols] = kk[HALF:]
        vv = dot_nn(p1[h], o1)
        cg[2, 0, :HALF, cols] = vv[:HALF] + dot_nn(p0[h], o0)
        cg[2, 1, :HALF, cols] = vv[HALF:]

    def taps(c, h):
        cols = cols_of(h)
        found = [jnp.zeros((8, HD), F32)] * TAPS
        for half in range(2):
            for lo in range(0, HALF, HD):
                grad = cg[c, half, pl.ds(lo, HD), cols]
                rows = xf[c, half, pl.ds(lo, LEAD + HD), cols]
                for j in range(TAPS):
                    part = grad * rows[LEAD - 8 * j : LEAD - 8 * j + HD]
                    found[j] = found[j] + jnp.sum(part.reshape(HD // 8, 8, HD), axis=0)
        for j in range(TAPS):
            r = j + TAPS * (c == 2)
            tap[int(c > 0), r : r + 1, cols] = jnp.sum(found[j], axis=0, keepdims=True)

    def q_taps(h, c):
        taps(0, h)
        cols = cols_of(h)
        tap[0, 4:5, cols] = jnp.sum(
            gf[:, cols] * (att[:, cols] * invb[...]), axis=0, keepdims=True
        )

    over(0, heads, back)
    over(0, heads // 4, q_taps)
    scan_slices(True, bs, b1_s, br, b1_r, bo, bi, b2_s, b2_r)

    def edge(c):
        return ctx_copy(
            etx.at[c], erx.at[c], eh_s.at[c], eh_r.at[c], lax.rem(me + n - 1, n)
        )

    def send_edge(c):
        for j in range(TAPS - 1):
            etx[c, j : j + 1, :] = cg[c, 0, pl.ds(8 * j, 1), :]

        @pl.when(me > 0)
        def _():
            edge(c).start()

    @pl.when(me == n - 1)
    def _():
        erx[...] = jnp.zeros_like(erx)

    send_edge(0)

    def kv_taps(h, c):
        taps(1, h)
        taps(2, h)

    over(heads // 4, heads, q_taps)

    def tap_pair(s):
        return ctx_copy(tap.at[s], tapp.at[s], tp_s.at[s], tp_r.at[s], partner)

    def tap_copy(s, p, source):
        return ctx_copy(tapb.at[s], tapr.at[s, source], t_s.at[s], t_r.at[s], p)

    def tap_all(s):
        rows = tapr.at[s, pl.ds(0, n - 1)]
        return ctx_copy(rows, rows, t_s.at[s], t_r.at[s], partner)

    own_cols = pl.ds(pl.multiple_of(mine * HD, HD), hc * HD)
    fold = hc * HD // 2 >= HD

    def send_taps(s, sums_):
        half = hc * HD // 2
        if fold:
            wide = jnp.concatenate([sums_[:, :half], sums_[:, half:]], axis=0)
        else:
            wide = jnp.concatenate([sums_, jnp.zeros_like(sums_)], axis=0)
        tapb[s] = wide.astype(BF16)
        everyone(lambda p: tap_copy(s, p, me).start())

    def contract(own_state, their_state, i):
        rows = []
        for a in range(2):
            own = own_state if a else own_state.T
            their = their_state if a else their_state.T
            for j in range(TAPS):
                part = pl.ds(j * HD, HD)
                both = own * wown[i, a, :, part] + their * wrx[i, a, :, part].astype(F32)
                rows.append(jnp.sum(both, axis=0, keepdims=True))
        return jnp.concatenate(rows, axis=0)

    tap_pair(0).start()
    over(0, heads, kv_taps)
    tap_pair(1).start()
    w_pair.wait_recv()

    tap_pair(0).wait_recv()
    send_taps(0, tap[0, :, own_cols] + tapp[0, :, own_cols])

    def edge_in(c):
        @pl.when(me < n - 1)
        def _():
            edge(c).wait_recv()

    def unconv(c, half):
        if half == 1:
            edge_in(c)
        for j in range(TAPS - 1):
            if half == 1:
                after = erx[c, j : j + 1, :]
            else:
                after = cg[c, 1, pl.ds(8 * j, 1), :]
            cg[c, half, pl.ds(HALF + 8 * j, 8), :] = jnp.where(
                last, jnp.broadcast_to(after, (8, width)), pltpu.roll(cg[c, half, pl.ds(8 * j, 8), :], 7, 0)
            )
        for k in range(0, width, chunk):
            cols = pl.ds(k, chunk)
            pieces = []
            for lo in range(0, HALF, HD // 2):
                rows = cg[c, half, pl.ds(lo, HD // 2 + LEAD), cols]
                y = w_ref[c, 0:1, cols] * rows[: HD // 2]
                for j in range(1, TAPS):
                    y = y + w_ref[c, j : j + 1, cols] * rows[8 * j : 8 * j + HD // 2]
                pieces.append(y.astype(BF16))
            outs[c][pl.ds(half * HALF, HALF), cols] = gather(jnp.concatenate(pieces, axis=0))

    outs = (qg_ref, kg_ref, vg_ref)
    tap_pair(1).wait_recv()
    tapl[...] = tap[1, :, own_cols] + tapp[1, :, own_cols]
    arrived(bi, b2_r, owners, lambda o: result_copy(bo, bi, b2_s, b2_r, 0, o).wait_recv())
    bp_in = pass_on(behind, bx_r, bi, bp, bin_, bp_s, bp_r)
    for i in range(hc):
        p = bi[pl.ds(i * per, per)].reshape(HD, HD).astype(F32)
        for_them = jnp.exp(closb[mine + i][0:1, :]) * p + local[mine + i]
        for_me = jnp.exp(closp[mine + i][0:1, :]) * p + bx_r[i].astype(F32)
        tapl[:, i * HD : (i + 1) * HD] += contract(
            jnp.where(behind, p, for_me), jnp.where(behind, for_them, p), i
        )
    send_taps(1, tapl[...])

    def late(lo, halves):
        def some(h, c):
            cols = cols_of(h)
            state = bin_[h]
            for half, start in halves:
                a, b = half * HALF + start, half * HALF + lo
                sh = shr[h, a:b]
                cg[1, half, start:lo, cols] += dot_nt(vc[a:b, cols], state) * sh
                cg[2, half, start:lo, cols] += dot_nn(kc[a:b, cols], state) * sh

        return some

    def early_rows(h, c):
        late(FIX, ((0, 0),))(h, c)

    def other_rows(h, c):
        late(HALF, ((0, FIX), (1, 0)))(h, c)

    group(mine, early_rows)
    for k in range(-(-width // 2 // chunk) * chunk, width, chunk):
        mixing(k)
    bp_in.wait_recv()
    group(theirs, early_rows)
    send_edge(1)
    send_edge(2)
    over(0, heads, other_rows)
    unconv(0, 0)
    unconv(0, 1)
    unconv(1, 0)
    unconv(2, 0)
    unconv(1, 1)
    unconv(2, 1)

    def sum_taps(s):
        tap_all(s).wait_recv()
        tapr[s, me] = tapb[s]
        found = []
        for g in range(2):
            wide = tapr[s, g].astype(F32)
            if chips <= UNROLL:
                for p in range(1, chips):
                    wide = wide + tapr[s, 2 * p + g].astype(F32)
            else:
                wide = lax.fori_loop(
                    1, chips, lambda p, a: a + tapr[s, 2 * p + g].astype(F32), wide
                )
            found.append(wide[:8])
            if fold:
                found.append(wide[8:])
        return jnp.concatenate(found, axis=1)

    q_sums = sum_taps(0)
    cgrad_ref[0] = q_sums[0:4]
    ggrad_ref[...] = q_sums[4:5]
    kv_sums = sum_taps(1)
    cgrad_ref[1] = kv_sums[0:4]
    cgrad_ref[2] = kv_sums[4:8]

    @pl.when(me < n - 1)
    def _():
        for c in range(3):
            halo(c).wait_send()

    @pl.when(me > 0)
    def _():
        for c in range(3):
            edge(c).wait_send()

    clos_pair.wait_send()
    w_pair.wait_send()
    fx.wait_send()
    bx.wait_send()
    fp_in.wait_send()
    bp_in.wait_send()

    def sent_to_owner(o):
        clos_copy(o, chip).wait_send()
        slice_copy(fs, fr, f1_s, f1_r, o, chip).wait_send()
        slice_copy(bs, br, b1_s, b1_r, o, chip).wait_send()

    def sent_states():
        def one(p):
            result_copy(fo, fi, f2_s, f2_r, p, chip).wait_send()
            result_copy(bo, bi, b2_s, b2_r, p, chip).wait_send()

        peers(chips, one)

    if single:
        for ref, sem in ((closr, cl_s), (fr, f1_s), (br, b1_s), (fi, f2_s), (bi, b2_s)):
            sent(ref, sem)
    else:
        peers(owners, sent_to_owner)
        owning(sent_states)
    for d in range(1, m):
        sums_copy(lax.rem(hme + d, m), hme).wait_send()
    for s in range(2):
        tap_pair(s).wait_send()
        tap_all(s).wait_send()


def hand_on(*refs):
    count = (len(refs) - 1) // 2
    put = refs[-1]
    moves = []
    for i in range(count):
        pieces = PIECES if i < 4 else 1
        for j in range(pieces):
            src, dst = refs[i], refs[count + i]
            if pieces > 1:
                part = pl.ds(j * (GROUP // pieces), GROUP // pieces)
                src, dst = src.at[part, :], dst.at[part, :]
            moves.append(pltpu.make_async_copy(src, dst, put.at[len(moves)]))
    for cp in moves:
        cp.start()
    for cp in moves:
        cp.wait()


def body(n, m, query_rows, key_rows, value_rows, log_gate, conv_weight, norm_gain, mixed_grad):
    tok_here, width = query_rows.shape
    assert tok_here == GROUP
    heads = width // HD
    chips = n // 2
    hc = heads // 2
    owners = min(chips, hc * HD // 16)
    R = hc * HD // owners
    if heads < 8:
        log_gate = jnp.pad(log_gate, ((0, 8 - heads), (0, 0)))
    any_ = pl.BlockSpec(memory_space=pl.ANY)
    vm = pl.BlockSpec(memory_space=pltpu.VMEM)
    V = pltpu.VMEM
    S = pltpu.SemaphoreType.DMA
    hbm = pl.BlockSpec(memory_space=pltpu.HBM)
    result = pl.pallas_call(
        functools.partial(kernel, n, m, heads, owners),
        out_shape=(
            V((GROUP, width), BF16), V((GROUP, width), BF16),
            V((GROUP, width), BF16), V((GROUP, width), BF16),
            V((3, TAPS, width), F32), V((1, width), F32),
        ),
        in_specs=[hbm] * 7,
        out_specs=(vm,) * 6,
        scratch_shapes=[
            V((4, GROUP, width), BF16),
            V((3, EDGE, width), BF16),
            V((8, GROUP), F32),
            V((3, TAPS, width), F32),
            V((1, width), F32),
            V((2, HALF, HALF), BF16),
            V((3, 2, LEAD + HALF, width), F32),
            V((GROUP, width), BF16),
            V((GROUP, width), BF16),
            V((GROUP, width), BF16),
            V((heads, HD, GROUP), BF16),
            V((GROUP, width), F32),
            V((GROUP, width), F32),
            V((GROUP, width), F32),
            V((GROUP, width), BF16),
            V((3, 2, HALF + LEAD, width), F32),
            V((3, 8, width), F32),
            V((3, 8, width), F32),
            V((heads, HALF, HALF), F32),
            V((heads, HALF, GROUP), F32),
            V((heads, HALF, HALF), BF16),
            V((heads, GROUP, HALF), BF16),
            V((heads, GROUP, HD), F32),
            V((heads, GROUP, HD), F32),
            V((heads, GROUP, HD), F32),
            V((heads, 8, GROUP), F32),
            V((heads, 8, HD), F32),
            V((heads, 8, HD), F32),
            V((hc, 8, HD), F32),
            V((chips, 8, HD), F32),
            V((2, GROUP, TAPS * HD), BF16),
            V((hc, 2, HD, TAPS * HD), F32),
            V((hc, 2, HD, TAPS * HD), BF16),
            V((hc, 2, HD, TAPS * HD), BF16),
            V((8, hc * HD), F32),
            V((heads, HD, HD), F32),
            V((hc, HD, HD), BF16),
            V((hc, HD, HD), BF16),
            V((owners, R, HD), BF16),
            V((chips, R, HD), BF16),
            V((chips, R, HD), BF16),
            V((owners, R, HD), BF16),
            V((hc, HD, HD), BF16),
            V((heads, HD, HD), BF16),
            V((hc, HD, HD), BF16),
            V((hc, HD, HD), BF16),
            V((owners, R, HD), BF16),
            V((chips, R, HD), BF16),
            V((chips, R, HD), BF16),
            V((owners, R, HD), BF16),
            V((hc, HD, HD), BF16),
            V((heads, HD, HD), BF16),
            V((GROUP, HD), F32),
            V((GROUP, HD), F32),
            V((GROUP, HD), F32),
            V((GROUP, HD), F32),
            V((8, HD), F32),
            V((m, 8, HD), F32),
            V((2, 8, width), F32),
            V((2, 8, width), F32),
            V((2, 16, max(hc * HD // 2, HD)), BF16),
            V((2, n, 16, max(hc * HD // 2, HD)), BF16),
            S((7,)), S((3,)), S((3,)), S((1,)), S((1,)), S((chips,)), S((chips,)),
            S((1,)), S((1,)), S((chips,)), S((chips,)), S((chips,)), S((chips,)), S((1,)), S((1,)),
            S((1,)), S((1,)), S((chips,)), S((chips,)), S((chips,)), S((chips,)), S((1,)), S((1,)),
            S((m,)), S((m,)), S((3,)), S((3,)), S((2,)), S((2,)), S((2,)), S((2,)), S((1,)), S((1,)),
        ],
        compiler_params=pltpu.CompilerParams(
            collective_id=0, has_side_effects=True, vmem_limit_bytes=56 * 1024 * 1024
        ),
    )(
        query_rows, key_rows, value_rows, mixed_grad,
        log_gate, conv_weight, norm_gain.reshape(1, width),
    )
    result = pl.pallas_call(
        hand_on,
        out_shape=tuple(jax.ShapeDtypeStruct(r.shape, r.dtype) for r in result),
        in_specs=[any_] * 6,
        out_specs=(any_,) * 6,
        scratch_shapes=[S((4 * PIECES + 2,))],
        compiler_params=pltpu.CompilerParams(vmem_limit_bytes=4 * 1024 * 1024),
    )(*result)
    return (*result[:5], result[5].reshape(width))


def solution(mesh):
    n, m = mesh.shape["ctx"], mesh.shape["head"]
    rows = P("ctx", "head")
    return jax.shard_map(
        functools.partial(body, n, m),
        mesh=mesh,
        in_specs=(rows, rows, rows, P("head", "ctx"), P(None, None, "head"), P("head"), rows),
        out_specs=(rows, rows, rows, rows, P(None, None, "head"), P("head")),
        check_vma=False,
    )
```

```python
import functools

import jax
import jax.numpy as jnp
from jax import lax
from jax.experimental import pallas as pl
from jax.experimental.pallas import tpu as pltpu
from jax.sharding import PartitionSpec as P

HD = 128
TAPS = 4
GROUP = 512
HALF = GROUP // 2
UNROLL = 8
SEG = HALF // 8
LEAD = 8 * (TAPS - 1)
EDGE = 16
FIX = 32
PIECES = 1
EPS = 1e-05
MESH = pl.DeviceIdType.MESH
F32 = jnp.float32
BF16 = jnp.bfloat16


def dot_nn(a, b):
    return lax.dot_general(a, b, (((1,), (0,)), ((), ())), preferred_element_type=F32)


def dot_nt(a, b):
    return lax.dot_general(a, b, (((1,), (1,)), ((), ())), preferred_element_type=F32)


def dot_tn(a, b):
    return lax.dot_general(a, b, (((0,), (0,)), ((), ())), preferred_element_type=F32)


def times(shape, axis):
    p = lax.broadcasted_iota(jnp.int32, shape, axis)
    return (p & 7) * SEG + (p >> 3)


def kernel(
    n, m, heads, owners,
    q_hbm, k_hbm, v_hbm, g_hbm, lg_hbm, w_hbm, gain_hbm,
    mix_ref, qg_ref, kg_ref, vg_ref, cgrad_ref, ggrad_ref,
    ext, hal, lg_ref, w_ref, gain_ref, perm,
    xf, qc, kc, vc, qsb, gf, ggf, att, og, cg, etx, erx,
    w0, w1, p0, p1, colb, grow, shr, rowb, closb, closp, closc, closr,
    x4, wown, wtx, wrx, tapl,
    local, fx_t, fx_r, fs, fr, fo, fi, fp, fin,
    bx_t, bx_r, bs, br, bo, bi, bp, bin_,
    accs, acci, invb, coefb, hs_tx, hs_rx,
    tap, tapp, tapb, tapr,
    loc, ha_s, ha_r, cp_s, cp_r, cl_s, cl_r,
    fx_s, fx_q, f1_s, f1_r, f2_s, f2_r, fp_s, fp_r,
    bx_s, bx_q, b1_s, b1_r, b2_s, b2_r, bp_s, bp_r,
    hs_s, hs_r, eh_s, eh_r, tp_s, tp_r, t_s, t_r, wp_s, wp_r,
):
    me = lax.axis_index("ctx")
    hme = lax.axis_index("head")
    chips = n // 2
    chip = me // 2
    core = lax.rem(me, 2)
    partner = me + 1 - 2 * core
    hc = heads // 2
    mine = core * hc
    theirs = hc - mine
    per = owners // hc
    R = HD // per
    width = heads * HD
    total = width * m
    convs = (qc, kc, vc)
    chunk = min(2 * HD, width)

    def ctx_copy(src, dst, ss, rs, p):
        return pltpu.make_async_remote_copy(
            src_ref=src, dst_ref=dst, send_sem=ss, recv_sem=rs,
            device_id={"ctx": p}, device_id_type=MESH,
        )

    def head_copy(src, dst, ss, rs, p):
        return pltpu.make_async_remote_copy(
            src_ref=src, dst_ref=dst, send_sem=ss, recv_sem=rs,
            device_id={"head": p}, device_id_type=MESH,
        )

    def peers(count, fn):
        def one(d, c):
            p = lax.rem(chip + d, chips)
            if count == chips:
                fn(p)
            else:
                pl.when(p < count)(lambda: fn(p))
            return c

        lax.fori_loop(1, chips, one, 0)

    def everyone(fn):
        def one(d, c):
            fn(lax.rem(me + d, n))
            return c

        lax.fori_loop(1, n, one, 0)

    single = owners == chips

    def slot(sem, i):
        return sem.at[0] if single else sem.at[i]

    def bulk(ref, count, sem):
        rows = ref.at[pl.ds(0, count)]
        return ctx_copy(rows, rows, sem.at[0], sem.at[0], partner)

    def arrived(ref, sem, count, one):
        if single:
            bulk(ref, chips - 1, sem).wait_recv()
        else:
            peers(count, one)

    def sent(ref, sem):
        bulk(ref, chips - 1, sem).wait_send()

    def owning(fn):
        if owners == chips:
            fn()
        else:
            pl.when(chip < owners)(fn)

    def cols_of(h):
        if isinstance(h, int):
            return pl.ds(h * HD, HD)
        return pl.ds(pl.multiple_of(h * HD, HD), HD)

    def over(lo, hi, fn):
        for h in range(lo, hi):
            fn(h, 0)

    def group(first, fn):
        for i in range(hc):
            fn(first + i, i)

    ins = [
        pltpu.make_async_copy(src, dst, loc.at[i])
        for i, (src, dst) in enumerate((
            (lg_hbm, lg_ref), (k_hbm, ext.at[1]), (v_hbm, ext.at[2]),
            (w_hbm, w_ref), (q_hbm, ext.at[0]), (g_hbm, ext.at[3]), (gain_hbm, gain_ref),
        ))
    ]
    for i in (0, 1, 2, 3, 6):
        ins[i].start()

    barrier = pltpu.get_barrier_semaphore()

    def greet(p):
        pl.semaphore_signal(barrier, inc=1, device_id={"ctx": p}, device_id_type=MESH)

    everyone(greet)
    for d in range(1, m):
        pl.semaphore_signal(
            barrier, inc=1, device_id={"head": lax.rem(hme + d, m)}, device_id_type=MESH
        )

    at = times((HALF, HALF), 0)
    along = times((HALF, HALF), 1)
    row_id = lax.broadcasted_iota(jnp.int32, (HALF, HALF), 0)
    lane_id = lax.broadcasted_iota(jnp.int32, (HALF, HALF), 1)
    perm[0] = jnp.where(at == lane_id, 1.0, 0.0).astype(BF16)
    perm[1] = jnp.where(row_id == along, 1.0, 0.0).astype(BF16)

    etx[...] = jnp.zeros_like(etx)
    tap[...] = jnp.zeros_like(tap)

    ins[0].wait()
    gate = lg_ref[...]
    high = gate.astype(BF16).astype(F32)
    rest = gate - high
    mid_ = rest.astype(BF16).astype(F32)
    parts = (high, mid_, rest - mid_)
    stacked = jnp.concatenate(
        [x[:, :HALF] for x in parts] + [x[:, HALF:] for x in parts], axis=0
    ).astype(BF16)
    upto = jnp.where(row_id <= along, 1.0, 0.0).astype(BF16)
    sums_ = dot_nn(stacked, upto)
    run0 = sums_[0:8] + sums_[8:16] + sums_[16:24]
    run1 = sums_[24:32] + sums_[32:40] + sums_[40:48] + run0[:, HALF - 1 : HALF]
    run = jnp.concatenate([run0, run1], axis=1)
    run_t = run.T
    for h in range(heads):
        colb[h] = jnp.broadcast_to(run_t[:, h : h + 1], (GROUP, HD))
        rowb[h] = jnp.broadcast_to(run[h : h + 1, :], (8, GROUP))
        closb[h] = jnp.broadcast_to(run[h : h + 1, GROUP - 1 : GROUP], (8, HD))

    def spread(c, i, dst):
        ins[i].wait()
        for half in range(2):
            for k in range(0, width, chunk):
                cols = pl.ds(k, chunk)
                dst(half)[:, cols] = dot_nn(perm[0], ext[c, pl.ds(half * HALF, HALF), cols])

    def gather(src):
        return dot_nn(perm[1], src).astype(BF16)

    first = lax.broadcasted_iota(jnp.int32, (8, width), 0) == 0
    last = lax.broadcasted_iota(jnp.int32, (8, width), 0) == 7

    def lead(c, half):
        if half == 0:
            edge_rows = hal[c].astype(F32)
        for j in range(1, TAPS):
            r = LEAD + HALF - 8 * j
            if half == 0:
                before = edge_rows[EDGE - j : EDGE - j + 1]
            else:
                before = xf[c, 0, pl.ds(r + 7, 1), :]
            xf[c, half, pl.ds(LEAD - 8 * j, 8), :] = jnp.where(
                first, jnp.broadcast_to(before, (8, width)), pltpu.roll(xf[c, half, pl.ds(r, 8), :], 1, 0)
            )

    def half_of(c):
        return lambda half: xf.at[c, half, pl.ds(LEAD, HALF), :]

    def conv(c, h, half, lo, count):
        cols = cols_of(h)
        end = lo + count
        while lo < end:
            now = min(HD - lo % HD, end - lo)
            rows = xf[c, half, pl.ds(lo, LEAD + now), cols]
            y = w_ref[c, 0:1, cols] * rows[LEAD:]
            for j in range(1, TAPS):
                y = y + w_ref[c, j : j + 1, cols] * rows[LEAD - 8 * j : LEAD - 8 * j + now]
            convs[c][pl.ds(half * HALF + lo, now), cols] = y.astype(BF16)
            lo += now

    def halo(c):
        return ctx_copy(
            (q_hbm, k_hbm, v_hbm)[c].at[pl.ds(GROUP - EDGE, EDGE), :], hal.at[c],
            ha_s.at[c], ha_r.at[c], lax.rem(me + 1, n),
        )

    spread(1, 1, half_of(1))
    clos_pair = ctx_copy(closb, closp, cp_s.at[0], cp_r.at[0], partner)
    pl.semaphore_wait(barrier, n - 1 + m - 1)

    @pl.when(me < n - 1)
    def _():
        for c in (1, 2, 0):
            halo(c).start()

    clos_pair.start()

    @pl.when(me == 0)
    def _():
        hal[...] = jnp.zeros_like(hal)

    spread(2, 2, half_of(2))
    ins[4].start()
    ins[5].start()
    ins[3].wait()
    lead(1, 1)
    lead(2, 1)

    def local_state(h, i):
        cols = cols_of(h)
        for c in (1, 2):
            conv(c, h, 0, FIX, HALF - FIX)
            conv(c, h, 1, 0, HALF)
        shr[h] = jnp.exp(closb[h][0:1, :] - colb[h])
        ks = (kc[FIX:, cols].astype(F32) * shr[h, FIX:]).astype(BF16)
        local[h] = dot_tn(ks, vc[FIX:, cols])

    group(theirs, local_state)
    group(mine, local_state)

    @pl.when(me > 0)
    def _():
        halo(1).wait_recv()
        halo(2).wait_recv()

    lead(1, 0)
    lead(2, 0)

    def whole_state(h):
        cols = cols_of(h)
        for c in (1, 2):
            conv(c, h, 0, 0, FIX)
        ks = (kc[:FIX, cols].astype(F32) * shr[h, :FIX]).astype(BF16)
        return local[h] + dot_tn(ks, vc[:FIX, cols])

    def their_state(h, i):
        fx_t[i] = whole_state(h).astype(BF16)

    group(theirs, their_state)
    fx = ctx_copy(fx_t, fx_r, fx_s.at[0], fx_q.at[0], partner)
    fx.start()

    def my_state(h, i):
        local[h] = whole_state(h)

    group(mine, my_state)

    def clos_copy(p, source):
        return ctx_copy(
            closc.at[p // per], closr.at[source], slot(cl_s, p), slot(cl_r, source), 2 * p + core
        )

    clos_pair.wait_recv()
    for i in range(hc):
        closc[i] = closb[mine + i] + closp[mine + i]
    peers(owners, lambda p: clos_copy(p, chip).start())

    def own_clos():
        closr[chip] = closc[chip // per]

    owning(own_clos)

    def decay(h, c):
        col = colb[h]
        grow[h] = jnp.exp(col)
        row = rowb[h][0:1, :]
        top = jnp.concatenate([col[:HALF]] * 2, axis=1)
        low = jnp.concatenate([col[HALF:]] * 2, axis=1)
        keep = times((HALF, HALF), 0) >= times((HALF, HALF), 1)
        w0[h] = jnp.where(keep, jnp.exp(jnp.minimum(top - row[:, :HALF], 0.0)), 0.0)
        w1[h, :, :HALF] = jnp.exp(jnp.minimum(low - row[:, :HALF], 0.0))
        w1[h, :, HALF:] = jnp.where(keep, jnp.exp(jnp.minimum(low - row[:, HALF:], 0.0)), 0.0)

    def slice_copy(src, dst, ss, rs, o, source):
        return ctx_copy(src.at[o], dst.at[source], slot(ss, o), slot(rs, source), 2 * o + core)

    def hand_out(leads, theirs_r, src, dst, ss, rs):
        for i in range(hc):
            a = jnp.where(leads, jnp.exp(closp[mine + i][0:1, :]), 1.0)
            b = jnp.where(leads, 1.0, jnp.exp(closb[mine + i][0:1, :]))
            both = (a * local[mine + i] + b * theirs_r[i].astype(F32)).astype(BF16)
            for k in range(per):
                src[i * per + k] = both[k * R : (k + 1) * R]
        peers(owners, lambda o: slice_copy(src, dst, ss, rs, o, chip).start())

        def keep():
            dst[chip] = src[chip]

        owning(keep)

    def scan_slices(backwards, src, ss, got, rs, out, res, ss2, rs2):
        def take():
            arrived(got, rs, chips, lambda s: slice_copy(src, got, ss, rs, 0, s).wait_recv())

            def step(i, state):
                b = chips - 1 - i if backwards else i
                out[b] = state.astype(BF16)
                return jnp.exp(closr[b][0:1, :]) * state + got[b].astype(F32)

            state = jnp.zeros((R, HD), F32)
            if chips <= UNROLL:
                for i in range(chips):
                    state = step(i, state)
            else:
                lax.fori_loop(0, chips, step, state)
            peers(chips, lambda p: result_copy(out, res, ss2, rs2, p, chip).start())
            res[chip] = out[chip]

        owning(take)

    def result_copy(out, res, ss2, rs2, p, source):
        return ctx_copy(
            out.at[p], res.at[source], slot(ss2, p), slot(rs2, source), 2 * p + core
        )

    def pass_on(leads, theirs_r, res, ptx, pin, ps, pr):
        for i in range(hc):
            p = res[pl.ds(i * per, per)].reshape(HD, HD).astype(F32)
            follow = jnp.exp(closb[mine + i][0:1, :]) * p + local[mine + i]
            ptx[i] = jnp.where(leads, follow, p).astype(BF16)
        copy = ctx_copy(ptx, pin.at[pl.ds(mine, hc)], ps.at[0], pr.at[0], partner)
        copy.start()
        for i in range(hc):
            p = res[pl.ds(i * per, per)].reshape(HD, HD).astype(F32)
            follow = jnp.exp(closp[mine + i][0:1, :]) * p + theirs_r[i].astype(F32)
            pin[mine + i] = jnp.where(leads, p, follow).astype(BF16)
        return ctx_copy(ptx, pin.at[pl.ds(theirs, hc)], ps.at[0], pr.at[0], partner)

    ahead = core == 0
    over(0, heads, decay)
    fx.wait_recv()
    hand_out(ahead, fx_r, fs, fr, f1_s, f1_r)

    spread(0, 4, half_of(0))

    @pl.when(me > 0)
    def _():
        halo(0).wait_recv()

    lead(0, 1)
    lead(0, 0)

    def inner(h, c):
        cols = cols_of(h)
        conv(0, h, 0, 0, HALF)
        conv(0, h, 1, 0, HALF)
        q0, q1 = qc[:HALF, cols], qc[HALF:, cols]
        a0 = (dot_nt(q0, kc[:HALF, cols]) * w0[h]).astype(BF16)
        a1 = (dot_nt(q1, kc[:, cols]) * w1[h]).astype(BF16)
        p0[h] = a0.T
        p1[h] = a1.T
        att[:HALF, cols] = dot_nn(a0, vc[:HALF, cols])
        att[HALF:, cols] = dot_nn(a1, vc[:, cols])
        qsb[h] = (qc[:, cols].astype(F32) * grow[h]).astype(BF16).T

    mid = max(heads * 3 // 4, 1)
    over(0, mid, inner)

    def clos_in():
        arrived(closr, cl_r, chips, lambda s: clos_copy(chip, s).wait_recv())

    owning(clos_in)
    scan_slices(False, fs, f1_s, fr, f1_r, fo, fi, f2_s, f2_r)
    over(mid, heads, inner)
    spread(3, 5, lambda half: gf.at[pl.ds(half * HALF, HALF), :])
    ins[6].wait()
    ggf[...] = gf[...] * gain_ref[...]

    def weigh(h):
        cols = cols_of(h)
        for i, src in ((1, vc), (2, kc)):
            for half in range(2):
                for lo in range(0, HALF, HD):
                    rows = xf[i, half, pl.ds(lo, LEAD + HD), cols]
                    for j in range(TAPS):
                        x4[i - 1, pl.ds(half * HALF + lo, HD), pl.ds(j * HD, HD)] = rows[
                            LEAD - 8 * j : LEAD - 8 * j + HD
                        ].astype(BF16)
            scaled = (src[:, cols].astype(F32) * shr[h]).astype(BF16)
            yield i - 1, dot_tn(scaled, x4[i - 1])

    def their_weights(h, i):
        for a, product in weigh(h):
            wtx[i, a] = product.astype(BF16)

    def my_weights(h, i):
        for a, product in weigh(h):
            wown[i, a] = product

    group(theirs, their_weights)
    w_pair = ctx_copy(wtx, wrx, wp_s.at[0], wp_r.at[0], partner)
    w_pair.start()
    arrived(fi, f2_r, owners, lambda o: result_copy(fo, fi, f2_s, f2_r, 0, o).wait_recv())
    fp_in = pass_on(ahead, fx_r, fi, fp, fin, fp_s, fp_r)


    def outer(h, c):
        cols = cols_of(h)
        a = att[:, cols] + dot_nn(qc[:, cols], fin[h]) * grow[h]
        att[:, cols] = a
        accs[...] += a * a
        acci[...] += ggf[:, cols] * a

    def outer_group(first_head, more):
        for lo in range(0, GROUP, HD):
            rows = pl.ds(lo, HD)
            square = accs[rows, :] if more else jnp.zeros((HD, HD), F32)
            inner_ = acci[rows, :] if more else jnp.zeros((HD, HD), F32)
            for i in range(hc):
                h = first_head + i
                cols = cols_of(h)
                a = att[rows, cols] + dot_nn(qc[rows, cols], fin[h]) * grow[h, rows]
                att[rows, cols] = a
                square = square + a * a
                inner_ = inner_ + ggf[rows, cols] * a
            accs[rows, :] = square
            acci[rows, :] = inner_

    outer_group(mine, False)
    fp_in.wait_recv()
    outer_group(theirs, True)
    for k, acc in ((0, accs), (4, acci)):
        row = jnp.sum(acc[...].T, axis=0, keepdims=True)
        for i in range(GROUP // HD):
            hs_tx[k + i : k + i + 1, :] = row[:, i * HD : (i + 1) * HD]

    def sums_copy(p, source):
        return head_copy(hs_tx, hs_rx.at[source], hs_s.at[p], hs_r.at[source], p)

    for d in range(1, m):
        sums_copy(lax.rem(hme + d, m), hme).start()
    hs_rx[hme] = hs_tx[...]
    group(mine, my_weights)
    for d in range(1, m):
        sums_copy(hme, lax.rem(hme + d, m)).wait_recv()
    sums = hs_rx[0]
    for d in range(1, m):
        sums = sums + hs_rx[d]
    inverse = lax.rsqrt(sums[0:4] / total + EPS)
    coef = inverse * inverse * (sums[4:8] / total)
    both = jnp.concatenate([inverse, coef], axis=0).T
    for i in range(GROUP // HD):
        rows = pl.ds(i * HD, HD)
        invb[rows, :] = jnp.broadcast_to(both[:, i : i + 1], (HD, HD))
        coefb[rows, :] = jnp.broadcast_to(both[:, 4 + i : 5 + i], (HD, HD))

    def norm(h, c):
        cols = cols_of(h)
        o = (invb[...] * (ggf[:, cols] - att[:, cols] * coefb[...])).astype(BF16)
        og[:, cols] = o
        return dot_nn(qsb[h], o)

    def their_norm(h, i):
        bx_t[i] = norm(h, i).astype(BF16)

    def my_norm(h, i):
        local[h] = norm(h, i)

    def mixing(k):
        cols = pl.ds(k, chunk)
        wide = jnp.concatenate([invb[...]] * (chunk // HD), axis=1)
        mixed = (att[:, cols] * wide * gain_ref[0:1, cols]).astype(BF16)
        for half in range(2):
            rows = pl.ds(half * HALF, HALF)
            mix_ref[rows, cols] = gather(mixed[half * HALF : (half + 1) * HALF])

    behind = core == 1
    group(theirs, their_norm)
    bx = ctx_copy(bx_t, bx_r, bx_s.at[0], bx_q.at[0], partner)
    bx.start()
    group(mine, my_norm)
    for k in range(0, width // 2, chunk):
        mixing(k)
    bx.wait_recv()
    hand_out(behind, bx_r, bs, br, b1_s, b1_r)

    def back(h, c):
        cols = cols_of(h)
        o0, o1 = og[:HALF, cols], og[HALF:, cols]
        s0 = (dot_nt(o0, vc[:HALF, cols]) * w0[h]).astype(BF16)
        s1 = (dot_nt(o1, vc[:, cols]) * w1[h]).astype(BF16)
        through = dot_nt(og[:, cols], fin[h]) * grow[h]
        cg[0, 0, :HALF, cols] = dot_nn(s0, kc[:HALF, cols]) + through[:HALF]
        cg[0, 1, :HALF, cols] = dot_nn(s1, kc[:, cols]) + through[HALF:]
        kk = dot_tn(s1, qc[HALF:, cols])
        cg[1, 0, :HALF, cols] = kk[:HALF] + dot_tn(s0, qc[:HALF, cols])
        cg[1, 1, :HALF, cols] = kk[HALF:]
        vv = dot_nn(p1[h], o1)
        cg[2, 0, :HALF, cols] = vv[:HALF] + dot_nn(p0[h], o0)
        cg[2, 1, :HALF, cols] = vv[HALF:]

    def taps(c, h):
        cols = cols_of(h)
        found = [jnp.zeros((8, HD), F32)] * TAPS
        for half in range(2):
            for lo in range(0, HALF, HD):
                grad = cg[c, half, pl.ds(lo, HD), cols]
                rows = xf[c, half, pl.ds(lo, LEAD + HD), cols]
                for j in range(TAPS):
                    part = grad * rows[LEAD - 8 * j : LEAD - 8 * j + HD]
                    found[j] = found[j] + jnp.sum(part.reshape(HD // 8, 8, HD), axis=0)
        for j in range(TAPS):
            r = j + TAPS * (c == 2)
            tap[int(c > 0), r : r + 1, cols] = jnp.sum(found[j], axis=0, keepdims=True)

    def q_taps(h, c):
        taps(0, h)
        cols = cols_of(h)
        tap[0, 4:5, cols] = jnp.sum(
            gf[:, cols] * (att[:, cols] * invb[...]), axis=0, keepdims=True
        )

    over(0, heads, back)
    over(0, heads // 4, q_taps)
    scan_slices(True, bs, b1_s, br, b1_r, bo, bi, b2_s, b2_r)

    def edge(c):
        return ctx_copy(
            etx.at[c], erx.at[c], eh_s.at[c], eh_r.at[c], lax.rem(me + n - 1, n)
        )

    def send_edge(c):
        for j in range(TAPS - 1):
            etx[c, j : j + 1, :] = cg[c, 0, pl.ds(8 * j, 1), :]

        @pl.when(me > 0)
        def _():
            edge(c).start()

    @pl.when(me == n - 1)
    def _():
        erx[...] = jnp.zeros_like(erx)

    send_edge(0)

    def kv_taps(h, c):
        taps(1, h)
        taps(2, h)

    over(heads // 4, heads, q_taps)

    def tap_pair(s):
        return ctx_copy(tap.at[s], tapp.at[s], tp_s.at[s], tp_r.at[s], partner)

    def tap_copy(s, p, source):
        return ctx_copy(tapb.at[s], tapr.at[s, source], t_s.at[s], t_r.at[s], p)

    def tap_all(s):
        rows = tapr.at[s, pl.ds(0, n - 1)]
        return ctx_copy(rows, rows, t_s.at[s], t_r.at[s], partner)

    own_cols = pl.ds(pl.multiple_of(mine * HD, HD), hc * HD)
    fold = hc * HD // 2 >= HD

    def send_taps(s, sums_):
        half = hc * HD // 2
        if fold:
            wide = jnp.concatenate([sums_[:, :half], sums_[:, half:]], axis=0)
        else:
            wide = jnp.concatenate([sums_, jnp.zeros_like(sums_)], axis=0)
        tapb[s] = wide.astype(BF16)
        everyone(lambda p: tap_copy(s, p, me).start())

    def contract(own_state, their_state, i):
        rows = []
        for a in range(2):
            own = own_state if a else own_state.T
            their = their_state if a else their_state.T
            for j in range(TAPS):
                part = pl.ds(j * HD, HD)
                both = own * wown[i, a, :, part] + their * wrx[i, a, :, part].astype(F32)
                rows.append(jnp.sum(both, axis=0, keepdims=True))
        return jnp.concatenate(rows, axis=0)

    tap_pair(0).start()
    over(0, heads, kv_taps)
    tap_pair(1).start()
    w_pair.wait_recv()

    tap_pair(0).wait_recv()
    send_taps(0, tap[0, :, own_cols] + tapp[0, :, own_cols])

    def edge_in(c):
        @pl.when(me < n - 1)
        def _():
            edge(c).wait_recv()

    def unconv(c, half):
        if half == 1:
            edge_in(c)
        for j in range(TAPS - 1):
            if half == 1:
                after = erx[c, j : j + 1, :]
            else:
                after = cg[c, 1, pl.ds(8 * j, 1), :]
            cg[c, half, pl.ds(HALF + 8 * j, 8), :] = jnp.where(
                last, jnp.broadcast_to(after, (8, width)), pltpu.roll(cg[c, half, pl.ds(8 * j, 8), :], 7, 0)
            )
        for k in range(0, width, chunk):
            cols = pl.ds(k, chunk)
            pieces = []
            for lo in range(0, HALF, HD // 2):
                rows = cg[c, half, pl.ds(lo, HD // 2 + LEAD), cols]
                y = w_ref[c, 0:1, cols] * rows[: HD // 2]
                for j in range(1, TAPS):
                    y = y + w_ref[c, j : j + 1, cols] * rows[8 * j : 8 * j + HD // 2]
                pieces.append(y.astype(BF16))
            outs[c][pl.ds(half * HALF, HALF), cols] = gather(jnp.concatenate(pieces, axis=0))

    outs = (qg_ref, kg_ref, vg_ref)
    tap_pair(1).wait_recv()
    tapl[...] = tap[1, :, own_cols] + tapp[1, :, own_cols]
    arrived(bi, b2_r, owners, lambda o: result_copy(bo, bi, b2_s, b2_r, 0, o).wait_recv())
    bp_in = pass_on(behind, bx_r, bi, bp, bin_, bp_s, bp_r)
    for i in range(hc):
        p = bi[pl.ds(i * per, per)].reshape(HD, HD).astype(F32)
        for_them = jnp.exp(closb[mine + i][0:1, :]) * p + local[mine + i]
        for_me = jnp.exp(closp[mine + i][0:1, :]) * p + bx_r[i].astype(F32)
        tapl[:, i * HD : (i + 1) * HD] += contract(
            jnp.where(behind, p, for_me), jnp.where(behind, for_them, p), i
        )
    send_taps(1, tapl[...])

    def late(lo, halves):
        def some(h, c):
            cols = cols_of(h)
            state = bin_[h]
            for half, start in halves:
                a, b = half * HALF + start, half * HALF + lo
                sh = shr[h, a:b]
                cg[1, half, start:lo, cols] += dot_nt(vc[a:b, cols], state) * sh
                cg[2, half, start:lo, cols] += dot_nn(kc[a:b, cols], state) * sh

        return some

    def early_rows(h, c):
        late(FIX, ((0, 0),))(h, c)

    def other_rows(h, c):
        late(HALF, ((0, FIX), (1, 0)))(h, c)

    group(mine, early_rows)
    for k in range(-(-width // 2 // chunk) * chunk, width, chunk):
        mixing(k)
    bp_in.wait_recv()
    group(theirs, early_rows)
    send_edge(1)
    send_edge(2)
    over(0, heads, other_rows)
    unconv(0, 0)
    unconv(0, 1)
    unconv(1, 0)
    unconv(2, 0)
    def sum_taps(s):
        tap_all(s).wait_recv()
        tapr[s, me] = tapb[s]
        found = []
        for g in range(2):
            wide = tapr[s, g].astype(F32)
            if chips <= UNROLL:
                for p in range(1, chips):
                    wide = wide + tapr[s, 2 * p + g].astype(F32)
            else:
                wide = lax.fori_loop(
                    1, chips, lambda p, a: a + tapr[s, 2 * p + g].astype(F32), wide
                )
            found.append(wide[:8])
            if fold:
                found.append(wide[8:])
        return jnp.concatenate(found, axis=1)

    q_sums = sum_taps(0)
    cgrad_ref[0] = q_sums[0:4]
    ggrad_ref[...] = q_sums[4:5]
    unconv(1, 1)
    unconv(2, 1)

    @pl.when(me < n - 1)
    def _():
        for c in range(3):
            halo(c).wait_send()

    @pl.when(me > 0)
    def _():
        for c in range(3):
            edge(c).wait_send()

    clos_pair.wait_send()
    w_pair.wait_send()
    fx.wait_send()
    bx.wait_send()
    fp_in.wait_send()
    bp_in.wait_send()

    def sent_to_owner(o):
        clos_copy(o, chip).wait_send()
        slice_copy(fs, fr, f1_s, f1_r, o, chip).wait_send()
        slice_copy(bs, br, b1_s, b1_r, o, chip).wait_send()

    def sent_states():
        def one(p):
            result_copy(fo, fi, f2_s, f2_r, p, chip).wait_send()
            result_copy(bo, bi, b2_s, b2_r, p, chip).wait_send()

        peers(chips, one)

    if single:
        for ref, sem in ((closr, cl_s), (fr, f1_s), (br, b1_s), (fi, f2_s), (bi, b2_s)):
            sent(ref, sem)
    else:
        peers(owners, sent_to_owner)
        owning(sent_states)
    for d in range(1, m):
        sums_copy(lax.rem(hme + d, m), hme).wait_send()
    kv_sums = sum_taps(1)
    cgrad_ref[1] = kv_sums[0:4]
    cgrad_ref[2] = kv_sums[4:8]

    for s in range(2):
        tap_pair(s).wait_send()
        tap_all(s).wait_send()


def hand_on(*refs):
    count = (len(refs) - 1) // 2
    put = refs[-1]
    moves = []
    for i in range(count):
        pieces = PIECES if i < 4 else 1
        for j in range(pieces):
            src, dst = refs[i], refs[count + i]
            if pieces > 1:
                part = pl.ds(j * (GROUP // pieces), GROUP // pieces)
                src, dst = src.at[part, :], dst.at[part, :]
            moves.append(pltpu.make_async_copy(src, dst, put.at[len(moves)]))
    for cp in moves:
        cp.start()
    for cp in moves:
        cp.wait()


def body(n, m, query_rows, key_rows, value_rows, log_gate, conv_weight, norm_gain, mixed_grad):
    tok_here, width = query_rows.shape
    assert tok_here == GROUP
    heads = width // HD
    chips = n // 2
    hc = heads // 2
    owners = min(chips, hc * HD // 16)
    R = hc * HD // owners
    if heads < 8:
        log_gate = jnp.pad(log_gate, ((0, 8 - heads), (0, 0)))
    any_ = pl.BlockSpec(memory_space=pl.ANY)
    vm = pl.BlockSpec(memory_space=pltpu.VMEM)
    V = pltpu.VMEM
    S = pltpu.SemaphoreType.DMA
    hbm = pl.BlockSpec(memory_space=pltpu.HBM)
    result = pl.pallas_call(
        functools.partial(kernel, n, m, heads, owners),
        out_shape=(
            V((GROUP, width), BF16), V((GROUP, width), BF16),
            V((GROUP, width), BF16), V((GROUP, width), BF16),
            V((3, TAPS, width), F32), V((1, width), F32),
        ),
        in_specs=[hbm] * 7,
        out_specs=(vm,) * 6,
        scratch_shapes=[
            V((4, GROUP, width), BF16),
            V((3, EDGE, width), BF16),
            V((8, GROUP), F32),
            V((3, TAPS, width), F32),
            V((1, width), F32),
            V((2, HALF, HALF), BF16),
            V((3, 2, LEAD + HALF, width), F32),
            V((GROUP, width), BF16),
            V((GROUP, width), BF16),
            V((GROUP, width), BF16),
            V((heads, HD, GROUP), BF16),
            V((GROUP, width), F32),
            V((GROUP, width), F32),
            V((GROUP, width), F32),
            V((GROUP, width), BF16),
            V((3, 2, HALF + LEAD, width), F32),
            V((3, 8, width), F32),
            V((3, 8, width), F32),
            V((heads, HALF, HALF), F32),
            V((heads, HALF, GROUP), F32),
            V((heads, HALF, HALF), BF16),
            V((heads, GROUP, HALF), BF16),
            V((heads, GROUP, HD), F32),
            V((heads, GROUP, HD), F32),
            V((heads, GROUP, HD), F32),
            V((heads, 8, GROUP), F32),
            V((heads, 8, HD), F32),
            V((heads, 8, HD), F32),
            V((hc, 8, HD), F32),
            V((chips, 8, HD), F32),
            V((2, GROUP, TAPS * HD), BF16),
            V((hc, 2, HD, TAPS * HD), F32),
            V((hc, 2, HD, TAPS * HD), BF16),
            V((hc, 2, HD, TAPS * HD), BF16),
            V((8, hc * HD), F32),
            V((heads, HD, HD), F32),
            V((hc, HD, HD), BF16),
            V((hc, HD, HD), BF16),
            V((owners, R, HD), BF16),
            V((chips, R, HD), BF16),
            V((chips, R, HD), BF16),
            V((owners, R, HD), BF16),
            V((hc, HD, HD), BF16),
            V((heads, HD, HD), BF16),
            V((hc, HD, HD), BF16),
            V((hc, HD, HD), BF16),
            V((owners, R, HD), BF16),
            V((chips, R, HD), BF16),
            V((chips, R, HD), BF16),
            V((owners, R, HD), BF16),
            V((hc, HD, HD), BF16),
            V((heads, HD, HD), BF16),
            V((GROUP, HD), F32),
            V((GROUP, HD), F32),
            V((GROUP, HD), F32),
            V((GROUP, HD), F32),
            V((8, HD), F32),
            V((m, 8, HD), F32),
            V((2, 8, width), F32),
            V((2, 8, width), F32),
            V((2, 16, max(hc * HD // 2, HD)), BF16),
            V((2, n, 16, max(hc * HD // 2, HD)), BF16),
            S((7,)), S((3,)), S((3,)), S((1,)), S((1,)), S((chips,)), S((chips,)),
            S((1,)), S((1,)), S((chips,)), S((chips,)), S((chips,)), S((chips,)), S((1,)), S((1,)),
            S((1,)), S((1,)), S((chips,)), S((chips,)), S((chips,)), S((chips,)), S((1,)), S((1,)),
            S((m,)), S((m,)), S((3,)), S((3,)), S((2,)), S((2,)), S((2,)), S((2,)), S((1,)), S((1,)),
        ],
        compiler_params=pltpu.CompilerParams(
            collective_id=0, has_side_effects=True, vmem_limit_bytes=56 * 1024 * 1024
        ),
    )(
        query_rows, key_rows, value_rows, mixed_grad,
        log_gate, conv_weight, norm_gain.reshape(1, width),
    )
    result = pl.pallas_call(
        hand_on,
        out_shape=tuple(jax.ShapeDtypeStruct(r.shape, r.dtype) for r in result),
        in_specs=[any_] * 6,
        out_specs=(any_,) * 6,
        scratch_shapes=[S((4 * PIECES + 2,))],
        compiler_params=pltpu.CompilerParams(vmem_limit_bytes=4 * 1024 * 1024),
    )(*result)
    return (*result[:5], result[5].reshape(width))


def solution(mesh):
    n, m = mesh.shape["ctx"], mesh.shape["head"]
    rows = P("ctx", "head")
    return jax.shard_map(
        functools.partial(body, n, m),
        mesh=mesh,
        in_specs=(rows, rows, rows, P("head", "ctx"), P(None, None, "head"), P("head"), rows),
        out_specs=(rows, rows, rows, rows, P(None, None, "head"), P("head")),
        check_vma=False,
    )
```
